512 devices in a mesh: dp: 64 (over y_lo, z, core), mp: 8 (over y_hi, x).
Axes of the slice: x: 4, y: 4 (y_hi: 2, y_lo: 2; y = y_hi * 2 + y_lo), z: 16, core: 2. Of those that a mesh axis runs over, the one named last changes fastest.
Arguments:
- acts: bfloat16 [16384, 28672], P('dp', 'mp'), may hold values from -24 to 24
- grads: bfloat16 [16384, 8192], P('dp', 'mp'), may hold values from -6 to 6
- basis_in: bfloat16 [28672, 640], P('mp', 'dp'), may hold values from -0.03125 to 0.03125
- basis_out: bfloat16 [8192, 1024], P('dp', 'mp'), may hold values from -0.0625 to 0.0625
- damping: float32 [1], replicated, may hold values from 0.5 to 2
Outputs:
- update: bfloat16 [28672, 8192], P('mp', 'dp')
- diag: float32 [640, 1024], P('mp', 'dp')
The draws below stay inside these ranges and needn't reach their ends.
All inputs are finite; a program needn't handle non-finite values.
Results may differ from the reference program's by a relative error of at most 0.0085.
Values may be sent and summed in bfloat16 or wider, within the bound.
A program may use at most 64 MiB of HBM per device.

```python
import math
import jax
import jax.numpy as jnp

DIN = 28672
DOUT = 8192
KA = 640
KG = 1024
TOKENS = 16384


def draw_acts(key, part):
    k_base, k_rows, k_cols = jax.random.split(key, 3)
    base = jax.random.normal(k_base, (TOKENS, DIN), jnp.float32)
    rows = jnp.exp(jax.random.uniform(k_rows, (TOKENS, 1), jnp.float32) * math.log(10.0)) / 4.6
    base = jnp.clip(base, -6.0, 6.0)
    cols = jnp.exp(jax.random.uniform(k_cols, (1, DIN), jnp.float32) * math.log(4.0)) / 2.3
    return (base * rows * cols).astype(jnp.bfloat16)


def levels(key, shape, cuts, least, top_value):
    loudness = 1.0
    for position, shards_of in cuts:
        steps = jax.random.uniform(jax.random.fold_in(jax.random.fold_in(key, 6), position), (shards_of,), jnp.float32, least / len(cuts), top_value / len(cuts))
        loudness = loudness * jnp.repeat(jnp.exp(steps), shape[position] // shards_of).reshape((-1,) + (1,) * (len(shape) - 1 - position))
    return loudness


def centred(key, dims, deviation, limit, cuts=(), dtype=jnp.bfloat16):
    loudness = levels(key, dims, cuts, -0.22, 0.18) if cuts else 1.0
    array = jax.random.normal(key, dims, jnp.float32) * deviation * loudness
    return jnp.minimum(jnp.maximum(array, -limit), limit).astype(dtype)


def setup_inputs(seed: int = 0) -> dict:
    arg_keys = jax.random.split(jax.random.key(seed), 6)
    return {
        "acts": draw_acts(jax.random.fold_in(arg_keys[5], 71), 0),
        "grads": centred(arg_keys[1], (TOKENS, DOUT), 1.0, 6.0, ((0, 64), (1, 8))),
        "basis_in": centred(arg_keys[2], (DIN, KA), DIN ** -0.5, 0.03125, ((0, 8), (1, 64))),
        "basis_out": centred(arg_keys[3], (DOUT, KG), DOUT ** -0.5, 0.0625, ((0, 64), (1, 8))),
        "damping": jnp.clip(jnp.exp(jax.random.uniform(arg_keys[4], (1,), jnp.float32, math.log(0.5), math.log(2.0))), 0.5, 2.0),
    }


def reference(acts, grads, basis_in, basis_out, damping):
    act_proj = jnp.dot(acts, basis_in, preferred_element_type=jnp.float32).astype(jnp.bfloat16)
    grad_proj = jnp.dot(grads, basis_out, preferred_element_type=jnp.float32).astype(jnp.bfloat16)
    act_sq = (act_proj.astype(jnp.float32) ** 2).astype(jnp.bfloat16)
    grad_sq = (grad_proj.astype(jnp.float32) ** 2).astype(jnp.bfloat16)
    grad_rot = jnp.dot(act_proj.T, grad_proj, preferred_element_type=jnp.float32)
    diag = jnp.dot(act_sq.T, grad_sq, preferred_element_type=jnp.float32) / TOKENS
    scaled = (grad_rot / (diag + damping[0])).astype(jnp.bfloat16)
    back = jnp.dot(scaled, basis_out.T, preferred_element_type=jnp.float32).astype(jnp.bfloat16)
    update = jnp.dot(basis_in, back, preferred_element_type=jnp.float32).astype(jnp.bfloat16)
    return update, diag
```

```python
import jax
import jax.numpy as jnp
from jax import lax
from jax.experimental import pallas as pl
from jax.experimental.pallas import tpu as pltpu
from jax.sharding import PartitionSpec as P

F32 = jnp.float32
BF16 = jnp.bfloat16
MESH = pl.DeviceIdType.MESH

NZ = 16
NQ = 4
NM = 8
KD = 10
KM = 80
NA = 256
NB = 768
HALF = NA + 2 * NB
LAG = 3


def kernel(
    tokens_all,
    acts, grads, bin_t, bout, damping,
    update, diag_t,
    qa, qb, mix, ga, gb, sb, bo, acc,
    snd_a, snd_g, rcv_a, rcv_g, act, gt, part, r1, p2, r2, sc, bk, bf,
    q_s, q_r, ra_s, ra_r, rb_s, rb_r, yb_s, yb_r, rs_s, rs_r, ys_s, ys_r,
    ca_s, ca_r, cb_s, cb_r, cs_s, cs_r, sw_s, sw_r, bo_s, bo_r,
    xa_s, xa_r, xg_s, xg_r, gt_s, gt_r, p1_s, p1_r, p2_s, p2_r,
    sz_s, sz_r, sq_s, sq_r, bk_s, bk_r,
):
    d = lax.axis_index("dp")
    m = lax.axis_index("mp")
    y = d // 32
    z = (d // 2) % 16
    c = d % 2
    oy = 1 - y
    oc = 1 - c
    me_q = 2 * y + c

    def dev(yy, zz, cc):
        return {"dp": yy * 32 + zz * 2 + cc, "mp": m}

    def copy(src, dst, ssem, rsem, device):
        return pltpu.make_async_remote_copy(
            src_ref=src, dst_ref=dst, send_sem=ssem, recv_sem=rsem,
            device_id=device, device_id_type=MESH,
        )

    here = {"dp": d, "mp": m}
    right = dev(y, (z + 1) % NZ, c)
    left = dev(y, (z + NZ - 1) % NZ, c)
    core = dev(y, z, oc)
    yside = dev(oy, z, c)
    quad = [(y, oc), (oy, c), (oy, oc)]
    swap_a = d // 8
    swap_d = 8 * m + d % 8
    far = swap_a != m

    barrier = pltpu.get_barrier_semaphore()

    def greet(device):
        pl.semaphore_signal(barrier, inc=1, device_id=device, device_id_type=MESH)

    for t in range(1, NZ):
        greet(dev(y, (z + t) % NZ, c))
    for yy, cc in quad:
        greet(dev(yy, z, cc))
    for t in range(1, NM):
        greet({"dp": d, "mp": (m + t) % NM})

    @pl.when(far)
    def _():
        greet({"dp": swap_d, "mp": swap_a})

    a_off = pl.multiple_of(c * HALF, 128)
    b_off = pl.multiple_of(c * HALF + NA + y * NB, 128)
    qa[me_q] = bin_t[:, pl.ds(a_off, NA)]
    qb[me_q] = bin_t[:, pl.ds(b_off, NB)]
    bo[m] = bout[...]

    @pl.when(jnp.logical_not(far))
    def _():
        sb[y, z, c] = bout[...]

    pl.semaphore_wait(barrier, NZ - 1 + 3 + NM - 1 + far.astype(jnp.int32))

    for n, (yy, cc) in enumerate(quad):
        a_to = pl.multiple_of(cc * HALF, 128)
        b_to = pl.multiple_of(cc * HALF + NA + yy * NB, 128)
        copy(bin_t.at[:, pl.ds(a_to, NA)], qa.at[me_q], q_s.at[n, 0], q_r.at[me_q, 0], dev(yy, z, cc)).start()
        copy(bin_t.at[:, pl.ds(b_to, NB)], qb.at[me_q], q_s.at[n, 1], q_r.at[me_q, 1], dev(yy, z, cc)).start()

    @pl.when(far)
    def _():
        copy(bout, sb.at[swap_d // 32, (swap_d // 2) % 16, swap_d % 2], sw_s, sw_r,
             {"dp": swap_d, "mp": swap_a}).start()

    for t in range(1, NM):
        copy(bout, bo.at[m], bo_s.at[t], bo_r.at[m], {"dp": d, "mp": (m + t) % NM}).start()

    for yy, cc in quad:
        s = 2 * yy + cc
        copy(qa.at[s], qa.at[s], q_s.at[0, 0], q_r.at[s, 0], here).wait_recv()
        copy(qb.at[s], qb.at[s], q_s.at[0, 1], q_r.at[s, 1], here).wait_recv()
    for s in range(NQ):
        mix[KD * s:KD * (s + 1), :NA] = qa[s].astype(F32)
        mix[KD * s:KD * (s + 1), NA:] = qb[s].astype(F32)
    ga[c, z] = mix[:40, :NA].astype(BF16)
    gb[c, y, z] = mix[:40, NA:].astype(BF16)

    def ring_a(zz, device):
        copy(ga.at[c, zz], ga.at[c, zz], ra_s, ra_r.at[zz], device).start()

    def ring_b(zz, device):
        copy(gb.at[c, y, zz], gb.at[c, y, zz], rb_s, rb_r.at[zz], device).start()

    def ring_s(yy, zz, device):
        copy(sb.at[yy, zz, c], sb.at[yy, zz, c], rs_s, rs_r.at[yy, zz], device).start()

    def core_a(zz):
        copy(ga.at[c, zz], ga.at[c, zz], ca_s, ca_r, core).start()

    def core_b(yy, zz):
        copy(gb.at[c, yy, zz], gb.at[c, yy, zz], cb_s, cb_r, core).start()

    def core_s(yy, zz):
        copy(sb.at[yy, zz, c], sb.at[yy, zz, c], cs_s, cs_r, core).start()

    def y_b(zz):
        copy(gb.at[c, y, zz], gb.at[c, y, zz], yb_s, yb_r.at[zz], yside).start()

    def got_a(zz):
        copy(ga.at[c, zz], ga.at[c, zz], ra_s, ra_r.at[zz], here).wait_recv()

    def got_b(zz):
        copy(gb.at[c, y, zz], gb.at[c, y, zz], rb_s, rb_r.at[zz], here).wait_recv()

    def got_s(yy, zz):
        copy(sb.at[yy, zz, c], sb.at[yy, zz, c], rs_s, rs_r.at[yy, zz], here).wait_recv()

    def got_y(zz):
        copy(gb.at[c, oy, zz], gb.at[c, oy, zz], yb_s, yb_r.at[zz], here).wait_recv()
        core_b(oy, zz)

    ring_b(z, right)
    ring_b(z, left)
    ring_a(z, right)
    ring_a(z, left)
    y_b(z)
    core_b(y, z)
    core_a(z)

    def step(s, _):
        zr = (z - s + NZ) % NZ
        zl = (z + s) % NZ

        @pl.when(s <= 8)
        def _():
            got_b(zr)

            @pl.when(s < 8)
            def _():
                ring_b(zr, right)

            y_b(zr)
            core_b(y, zr)

            @pl.when(s < 8)
            def _():
                got_b(zl)

                @pl.when(s < 7)
                def _():
                    ring_b(zl, left)

                y_b(zl)
                core_b(y, zl)

            got_a(zr)

            @pl.when(s < 8)
            def _():
                ring_a(zr, right)

            core_a(zr)

            @pl.when(s < 8)
            def _():
                got_a(zl)

                @pl.when(s < 7)
                def _():
                    ring_a(zl, left)

                core_a(zl)

        @pl.when(s == LAG)
        def _():
            @pl.when(far)
            def _():
                copy(sb.at[y, z, c], sb.at[y, z, c], sw_s, sw_r, here).wait_recv()

            copy(sb.at[y, z, c], sb.at[y, z, c], ys_s, ys_r, yside).start()
            ring_s(y, z, right)
            ring_s(y, z, left)
            core_s(y, z)
            copy(sb.at[oy, z, c], sb.at[oy, z, c], ys_s, ys_r, here).wait_recv()
            ring_s(oy, z, right)
            ring_s(oy, z, left)
            core_s(oy, z)

        @pl.when(s > LAG)
        def _():
            t = s - LAG
            sr = (z - t + NZ) % NZ
            sl = (z + t) % NZ
            for yy in (y, oy):
                got_s(yy, sr)

                @pl.when(t < 8)
                def _():
                    ring_s(yy, sr, right)

                core_s(yy, sr)

                @pl.when(t < 8)
                def _():
                    got_s(yy, sl)

                    @pl.when(t < 7)
                    def _():
                        ring_s(yy, sl, left)

                    core_s(yy, sl)

        @pl.when(s <= 9)
        def _():
            t = s - 1
            got_y((z - t + NZ) % NZ)

            @pl.when((t > 0) & (t < 8))
            def _():
                got_y((z + t) % NZ)

        return 0

    lax.fori_loop(1, 9 + LAG, step, 0)

    copy(ga.at[oc], ga.at[oc], ca_s, ca_r, here).wait_recv()
    copy(gb.at[oc], gb.at[oc], cb_s, cb_r, here).wait_recv()

    first = True
    for cc in range(2):
        for off, piece, width in (
            (cc * HALF, ga.at[cc], NA),
            (cc * HALF + NA, gb.at[cc, 0], NB),
            (cc * HALF + NA + NB, gb.at[cc, 1], NB),
        ):
            for k in range(0, width, 256):
                lhs = piece[:, :, k:k + 256].reshape(NZ * 40, 256)
                prod = lax.dot_general(
                    lhs, acts[:, off + k:off + k + 256], (((1,), (1,)), ((), ())),
                    preferred_element_type=F32,
                )
                if first:
                    acc[...] = prod
                    first = False
                else:
                    acc[...] += prod
    for mm in range(NM):
        yy, z0 = mm // 4, 4 * (mm % 4)
        for i in range(4):
            src = 40 * (z0 + i) + 20 * yy
            mix[20 * i:20 * (i + 1), :256] = acc[src:src + 20, :]
        snd_a[mm] = mix[:KM, :256].astype(BF16)
    for t in range(1, NM):
        to = (m + t) % NM
        copy(snd_a.at[to], rcv_a.at[m], xa_s.at[t], xa_r.at[m], {"dp": d, "mp": to}).start()
    rcv_a[m] = snd_a[m]

    copy(sb.at[:, :, oc], sb.at[:, :, oc], cs_s, cs_r, here).wait_recv()
    for mm in range(NM):
        yy, z0 = mm // 4, 4 * (mm % 4)
        block = sb[yy, z0:z0 + 4].reshape(1024, 128)
        snd_g[mm] = jnp.dot(grads[...], block, preferred_element_type=F32).astype(BF16)
    for t in range(1, NM):
        to = (m + t) % NM
        copy(snd_g.at[to], rcv_g.at[m], xg_s.at[t], xg_r.at[m], {"dp": d, "mp": to}).start()
    rcv_g[m] = snd_g[m]

    for t in range(1, NM):
        s = (m + t) % NM
        copy(rcv_a.at[s], rcv_a.at[s], xa_s.at[t], xa_r.at[s], here).wait_recv()
    total = rcv_a[0].astype(F32)
    for s in range(1, NM):
        total += rcv_a[s].astype(F32)
    act[...] = jnp.zeros_like(act)
    act[:KM, :] = total.astype(BF16)

    for t in range(1, NM):
        s = (m + t) % NM
        copy(rcv_g.at[s], rcv_g.at[s], xg_s.at[t], xg_r.at[s], here).wait_recv()
    total = rcv_g[0].astype(F32)
    for s in range(1, NM):
        total += rcv_g[s].astype(F32)
    gt[m] = total.T.astype(BF16)
    for t in range(1, NM):
        to = (m + t) % NM
        copy(gt.at[m], gt.at[m], gt_s.at[t], gt_r.at[m], {"dp": d, "mp": to}).start()
    for t in range(1, NM):
        s = (m + t) % NM
        copy(gt.at[s], gt.at[s], gt_s.at[t], gt_r.at[s], here).wait_recv()

    nt = (((1,), (1,)), ((), ()))
    a_val = act[...]
    a_sq = (a_val.astype(F32) ** 2).astype(BF16)
    for mm in range(NM):
        yy, z0 = mm // 4, 4 * (mm % 4)
        g_val = gt[mm]
        g_sq = (g_val.astype(F32) ** 2).astype(BF16)
        rot = lax.dot_general(g_val, a_val, nt, preferred_element_type=F32).astype(BF16)
        sq = lax.dot_general(g_sq, a_sq, nt, preferred_element_type=F32).astype(BF16)
        for i in range(8):
            part[yy, z0 + i // 2, i % 2, 0] = rot[16 * i:16 * (i + 1), :]
            part[yy, z0 + i // 2, i % 2, 1] = sq[16 * i:16 * (i + 1), :]
    for n, (yy, cc) in enumerate(quad):
        copy(part.at[yy, :, cc], r1.at[me_q], p1_s.at[n], p1_r.at[me_q], dev(yy, z, cc)).start()
    r1[me_q] = part[y, :, c]
    for yy, cc in quad:
        s = 2 * yy + cc
        copy(r1.at[s], r1.at[s], p1_s.at[0], p1_r.at[s], here).wait_recv()
    total = r1[0].astype(F32)
    for s in range(1, NQ):
        total += r1[s].astype(F32)
    p2[...] = total.astype(BF16)
    for t in range(1, NZ):
        to = (z + t) % NZ
        copy(p2.at[to], r2.at[z], p2_s.at[t], p2_r.at[z], dev(y, to, c)).start()
    r2[z] = p2[z]
    for t in range(1, NZ):
        s = (z + t) % NZ
        copy(r2.at[s], r2.at[s], p2_s.at[t], p2_r.at[s], here).wait_recv()
    total = r2[0].astype(F32)
    for s in range(1, NZ):
        total += r2[s].astype(F32)
    diag = total[1] / tokens_all
    diag_t[...] = diag[:, :KM]
    sc[y, z, c] = (total[0] / (diag + damping[0])).astype(BF16)

    for t in range(1, NZ):
        copy(sc.at[y, z, c], sc.at[y, z, c], sz_s.at[t], sz_r.at[z], dev(y, (z + t) % NZ, c)).start()
    for t in range(1, NZ):
        s = (z + t) % NZ
        copy(sc.at[y, s, c], sc.at[y, s, c], sz_s.at[t], sz_r.at[s], here).wait_recv()
    for n, (yy, cc) in enumerate(quad):
        copy(sc.at[y, :, c], sc.at[y, :, c], sq_s.at[n], sq_r.at[me_q], dev(yy, z, cc)).start()
    for yy, cc in quad:
        copy(sc.at[yy, :, cc], sc.at[yy, :, cc], sq_s.at[0], sq_r.at[2 * yy + cc], here).wait_recv()
    for t in range(1, NM):
        s = (m + t) % NM
        copy(bo.at[s], bo.at[s], bo_s.at[t], bo_r.at[s], here).wait_recv()

    total = jnp.zeros((128, 128), F32)
    for mm in range(NM):
        yy, z0 = mm // 4, 4 * (mm % 4)
        total += jnp.dot(bo[mm], sc[yy, z0:z0 + 4].reshape(128, 128), preferred_element_type=F32)
    bk[m] = total.T[:KM, :].astype(BF16)
    for t in range(1, NM):
        copy(bk.at[m], bk.at[m], bk_s.at[t], bk_r.at[m], {"dp": d, "mp": (m + t) % NM}).start()
    for t in range(1, NM):
        s = (m + t) % NM
        copy(bk.at[s], bk.at[s], bk_s.at[t], bk_r.at[s], here).wait_recv()
    for mm in range(NM):
        yy, z0 = mm // 4, 4 * (mm % 4)
        b_val = bk[mm].astype(F32)
        for i in range(4):
            dst = 40 * (z0 + i) + 20 * yy
            bf[dst:dst + 20, :] = b_val[20 * i:20 * (i + 1), :]
    back_t = bf[...].T.astype(BF16)
    for cc in range(2):
        for off, piece, width in (
            (cc * HALF, ga.at[cc], NA),
            (cc * HALF + NA, gb.at[cc, 0], NB),
            (cc * HALF + NA + NB, gb.at[cc, 1], NB),
        ):
            for k in range(0, width, 256):
                rhs = piece[:, :, k:k + 256].reshape(NZ * 40, 256)
                up = jnp.dot(back_t, rhs, preferred_element_type=F32)
                update[off + k:off + k + 256, :] = up.T.astype(BF16)

    for n in range(3):
        copy(qa.at[0], qa.at[0], q_s.at[n, 0], q_r.at[0, 0], here).wait_send()
        copy(qb.at[0], qb.at[0], q_s.at[n, 1], q_r.at[0, 0], here).wait_send()
        copy(r1.at[0], r1.at[0], p1_s.at[n], p1_r.at[0], here).wait_send()
        copy(sc.at[y, :, c], sc.at[y, :, c], sq_s.at[n], sq_r.at[0], here).wait_send()

    @pl.when(far)
    def _():
        copy(bout, bout, sw_s, sw_r, here).wait_send()

    for t in range(1, NM):
        copy(bout, bout, bo_s.at[t], bo_r.at[0], here).wait_send()
        copy(snd_a.at[0], snd_a.at[0], xa_s.at[t], xa_r.at[0], here).wait_send()
        copy(snd_g.at[0], snd_g.at[0], xg_s.at[t], xg_r.at[0], here).wait_send()
        copy(gt.at[0], gt.at[0], gt_s.at[t], gt_r.at[0], here).wait_send()
        copy(bk.at[0], bk.at[0], bk_s.at[t], bk_r.at[0], here).wait_send()
    for t in range(1, NZ):
        copy(p2.at[0], p2.at[0], p2_s.at[t], p2_r.at[0], here).wait_send()
        copy(sc.at[0, 0, 0], sc.at[0, 0, 0], sz_s.at[t], sz_r.at[0], here).wait_send()
    copy(ga.at[0, pl.ds(0, 15)], ga.at[0, pl.ds(0, 15)], ra_s, ra_r.at[0], here).wait_send()
    copy(gb.at[0, 0, pl.ds(0, 15)], gb.at[0, 0, pl.ds(0, 15)], rb_s, rb_r.at[0], here).wait_send()
    copy(gb.at[0, 0], gb.at[0, 0], yb_s, yb_r.at[0], here).wait_send()
    copy(sb.at[:, pl.ds(0, 15), 0], sb.at[:, pl.ds(0, 15), 0], rs_s, rs_r.at[0, 0], here).wait_send()
    copy(sb.at[0, 0, 0], sb.at[0, 0, 0], ys_s, ys_r, here).wait_send()
    copy(ga.at[0], ga.at[0], ca_s, ca_r, here).wait_send()
    copy(gb.at[0], gb.at[0], cb_s, cb_r, here).wait_send()
    copy(sb.at[:, :, 0], sb.at[:, :, 0], cs_s, cs_r, here).wait_send()


def solution(mesh):
    def on_device(acts, grads, basis_in, basis_out, damping):
        tokens_all = acts.shape[0] * mesh.shape["dp"]
        vmem = pl.BlockSpec(memory_space=pltpu.VMEM)
        dma = pltpu.SemaphoreType.DMA
        v = pltpu.VMEM

        def body(*refs):
            kernel(tokens_all, *refs)

        update, diag_t = pl.pallas_call(
            body,
            out_shape=(
                jax.ShapeDtypeStruct((3584, 128), BF16),
                jax.ShapeDtypeStruct((16, KM), F32),
            ),
            in_specs=[vmem] * 4 + [pl.BlockSpec(memory_space=pltpu.SMEM)],
            out_specs=(vmem, vmem),
            scratch_shapes=[
                v((NQ, KD, NA), BF16), v((NQ, KD, NB), BF16), v((KM, NA + NB), F32),
                v((2, NZ, 40, NA), BF16), v((2, 2, NZ, 40, NB), BF16),
                v((2, NZ, 2, 128, 128), BF16), v((NM, 128, 128), BF16), v((640, 256), F32),
                v((NM, KM, 256), BF16), v((NM, 256, 128), BF16),
                v((NM, KM, 256), BF16), v((NM, 256, 128), BF16),
                v((128, 256), BF16), v((NM, 128, 256), BF16),
                v((2, NZ, 2, 2, 16, 128), BF16), v((NQ, NZ, 2, 16, 128), BF16),
                v((NZ, 2, 16, 128), BF16), v((NZ, 2, 16, 128), BF16),
                v((2, NZ, 2, 16, 128), BF16), v((NM, KM, 128), BF16), v((640, 128), F32),
                dma((3, 2)), dma((NQ, 2)), dma, dma((NZ,)), dma, dma((NZ,)), dma, dma((NZ,)),
                dma, dma((2, NZ)), dma, dma,
                dma, dma, dma, dma, dma, dma, dma, dma, dma((NM,)), dma((NM,)),
                dma((NM,)), dma((NM,)), dma((NM,)), dma((NM,)), dma((NM,)), dma((NM,)),
                dma((3,)), dma((NQ,)), dma((NZ,)), dma((NZ,)),
                dma((NZ,)), dma((NZ,)), dma((3,)), dma((NQ,)), dma((NM,)), dma((NM,)),
            ],
            compiler_params=pltpu.CompilerParams(
                collective_id=0, has_side_effects=True, vmem_limit_bytes=48 * 2**20
            ),
        )(acts, grads, basis_in.T, basis_out, damping)
        return update, diag_t.T

    placed = (P("dp", "mp"), P("dp", "mp"), P("mp", "dp"), P("dp", "mp"), P())
    return jax.shard_map(
        on_device,
        mesh=mesh,
        in_specs=placed,
        out_specs=(P("mp", "dp"), P("mp", "dp")),
        check_vma=False,
    )
```

```python
import jax
import jax.numpy as jnp
from jax import lax
from jax.experimental import pallas as pl
from jax.experimental.pallas import tpu as pltpu
from jax.sharding import PartitionSpec as P

F32 = jnp.float32
BF16 = jnp.bfloat16
MESH = pl.DeviceIdType.MESH

NZ = 16
NQ = 4
NM = 8
KD = 10
KM = 80
NA = 1024
NB = 384
HALF = NA + 2 * NB
SLAG = 1
NC = 4
YLAG = 2


def kernel(
    tokens_all,
    acts_h, grads_h, bin_t, bout, damping,
    update, diag_t,
    acts, grads,
    qa, qb, mix, ga, gb, sb, bo, acc,
    snd_a, snd_g, rcv_a, rcv_g, act, own_g, gt, part, r1, p2, r2, sc, bk, bf,
    q_s, q_r, ra_s, ra_r, rb_s, rb_r, yb_s, yb_r, rs_s, rs_r, ys_s, ys_r,
    ca_s, ca_r, cb_s, cb_r, cs_s, cs_r, sw_s, sw_r, bo_s, bo_r,
    xa_s, xa_r, xg_s, xg_r, gt_s, gt_r, p1_s, p1_r, p2_s, p2_r,
    sz_s, sz_r, sq_s, sq_r, bk_s, bk_r, in_s, ac_s, ac_r,
):
    d = lax.axis_index("dp")
    m = lax.axis_index("mp")
    y = d // 32
    z = (d // 2) % 16
    c = d % 2
    oy = 1 - y
    oc = 1 - c
    me_q = 2 * y + c
    d_other = d + 1 - 2 * c

    def dev(yy, zz, cc):
        return {"dp": yy * 32 + zz * 2 + cc, "mp": m}

    def copy(src, dst, ssem, rsem, device):
        return pltpu.make_async_remote_copy(
            src_ref=src, dst_ref=dst, send_sem=ssem, recv_sem=rsem,
            device_id=device, device_id_type=MESH,
        )

    here = {"dp": d, "mp": m}
    right = dev(y, (z + 1) % NZ, c)
    left = dev(y, (z + NZ - 1) % NZ, c)
    core = dev(y, z, oc)
    yside = dev(oy, z, c)
    quad = [(y, oc), (oy, c), (oy, oc)]
    swap_a = d // 8
    swap_d = 8 * m + d % 8
    far = swap_a != m

    act[:, KM:, :] = jnp.zeros((2, 128 - KM, 256), BF16)
    barrier = pltpu.get_barrier_semaphore()

    def greet(device):
        pl.semaphore_signal(barrier, inc=1, device_id=device, device_id_type=MESH)

    for t in range(1, NZ):
        greet(dev(y, (z + t) % NZ, c))
    for yy, cc in quad:
        greet(dev(yy, z, cc))
    for t in range(1, NM):
        greet({"dp": d, "mp": (m + t) % NM})
        greet({"dp": d_other, "mp": (m + t) % NM})

    @pl.when(far)
    def _():
        greet({"dp": swap_d, "mp": swap_a})

    a_off = pl.multiple_of(c * HALF, 128)
    b_off = pl.multiple_of(c * HALF + NA + y * NB, 128)
    own_a = pltpu.make_async_copy(bin_t.at[:, pl.ds(a_off, NA)], qa.at[me_q], in_s.at[0])
    own_b = pltpu.make_async_copy(bin_t.at[:, pl.ds(b_off, NB)], qb.at[me_q], in_s.at[1])
    own_o = pltpu.make_async_copy(bout, bo.at[m], in_s.at[2])
    own_s = pltpu.make_async_copy(bout, sb.at[y, z, c], in_s.at[3])
    get_g = pltpu.make_async_copy(grads_h, grads, in_s.at[4])
    get_a = pltpu.make_async_copy(acts_h, acts, in_s.at[5])
    own_a.start()
    own_b.start()
    own_o.start()

    @pl.when(jnp.logical_not(far))
    def _():
        own_s.start()

    get_g.start()
    get_a.start()
    pl.semaphore_wait(barrier, NZ - 1 + 3 + 2 * (NM - 1) + far.astype(jnp.int32))

    @pl.when(far)
    def _():
        copy(bout, sb.at[swap_d // 32, (swap_d // 2) % 16, swap_d % 2], sw_s, sw_r,
             {"dp": swap_d, "mp": swap_a}).start()

    for yy, cc in quad:
        a_to = pl.multiple_of(cc * HALF, 128)
        b_to = pl.multiple_of(cc * HALF + NA + yy * NB, 128)
        copy(bin_t.at[:, pl.ds(a_to, NA)], qa.at[me_q], q_s.at[0], q_r.at[0], dev(yy, z, cc)).start()
        copy(bin_t.at[:, pl.ds(b_to, NB)], qb.at[me_q], q_s.at[1], q_r.at[1], dev(yy, z, cc)).start()
    for t in range(1, NM):
        copy(bout, bo.at[m], bo_s, bo_r, {"dp": d, "mp": (m + t) % NM}).start()

    def ring_a(q):
        def send(zz, device):
            copy(ga.at[c, q, zz], ga.at[c, q, zz], ra_s, ra_r.at[q, zz], device).start()

        return send

    def ring_b(zz, device):
        copy(gb.at[c, y, zz], gb.at[c, y, zz], rb_s, rb_r.at[zz], device).start()

    def ring_s(zz, device):
        copy(sb.at[y, zz, c], sb.at[y, zz, c], rs_s, rs_r.at[zz], device).start()

    def side_b(zz):
        copy(gb.at[c, y, zz], gb.at[c, y, zz], yb_s, yb_r.at[zz], yside).start()
        core_b(y, zz)

    def side_s(zz):
        copy(sb.at[y, zz, c], sb.at[y, zz, c], ys_s, ys_r.at[zz], yside).start()
        core_s(y, zz)

    def core_a(q):
        def send(zz):
            copy(ga.at[c, q, zz], ga.at[c, q, zz], ca_s, ca_r, core).start()

        return send

    def core_b(yy, zz):
        copy(gb.at[c, yy, zz], gb.at[c, yy, zz], cb_s, cb_r, core).start()

    def core_s(yy, zz):
        copy(sb.at[yy, zz, c], sb.at[yy, zz, c], cs_s, cs_r.at[yy], core).start()

    def got_a(q):
        def wait(zz):
            copy(ga.at[c, q, zz], ga.at[c, q, zz], ra_s, ra_r.at[q, zz], here).wait_recv()

        return wait

    def got_b(zz):
        copy(gb.at[c, y, zz], gb.at[c, y, zz], rb_s, rb_r.at[zz], here).wait_recv()

    def got_s(zz):
        copy(sb.at[y, zz, c], sb.at[y, zz, c], rs_s, rs_r.at[zz], here).wait_recv()

    def got_yb(zz):
        copy(gb.at[c, oy, zz], gb.at[c, oy, zz], yb_s, yb_r.at[zz], here).wait_recv()
        core_b(oy, zz)

    def got_ys(zz):
        copy(sb.at[oy, zz, c], sb.at[oy, zz, c], ys_s, ys_r.at[zz], here).wait_recv()
        core_s(oy, zz)

    own_a.wait()
    own_b.wait()
    copy(qa.at[:3], qa.at[:3], q_s.at[0], q_r.at[0], here).wait_recv()
    copy(qb.at[:3], qb.at[:3], q_s.at[1], q_r.at[1], here).wait_recv()
    for s in range(NQ):
        mix[KD * s:KD * (s + 1), :NA] = qa[s].astype(F32)
        mix[KD * s:KD * (s + 1), NA:] = qb[s].astype(F32)
    for q in range(NC):
        ga[c, q, z] = mix[:40, 256 * q:256 * (q + 1)].astype(BF16)
    gb[c, y, z] = mix[:40, NA:].astype(BF16)

    for q in range(NC):
        ring_a(q)(z, right)
        ring_a(q)(z, left)
        core_a(q)(z)
    ring_b(z, right)
    ring_b(z, left)
    side_b(z)

    def hop(t, got, ring, side):
        zr = (z - t + NZ) % NZ
        zl = (z + t) % NZ
        got(zr)

        @pl.when(t < 8)
        def _():
            ring(zr, right)

        side(zr)

        @pl.when(t < 8)
        def _():
            got(zl)

            @pl.when(t < 7)
            def _():
                ring(zl, left)

            side(zl)

    def side_hop(t, got):
        got((z - t + NZ) % NZ)

        @pl.when((t > 0) & (t < 8))
        def _():
            got((z + t) % NZ)

    def step(s, _):
        @pl.when(s <= 8)
        def _():
            for q in range(NC):
                hop(s, got_a(q), ring_a(q), core_a(q))
            hop(s, got_b, ring_b, side_b)

        @pl.when(s == SLAG)
        def _():
            @pl.when(far)
            def _():
                copy(sb.at[y, z, c], sb.at[y, z, c], sw_s, sw_r, here).wait_recv()

            @pl.when(jnp.logical_not(far))
            def _():
                own_s.wait()

            ring_s(z, right)
            ring_s(z, left)
            side_s(z)

        @pl.when((s > SLAG) & (s <= SLAG + 8))
        def _():
            hop(s - SLAG, got_s, ring_s, side_s)

        @pl.when((s >= YLAG) & (s <= YLAG + 8))
        def _():
            side_hop(s - YLAG, got_yb)

        @pl.when(s >= SLAG + YLAG)
        def _():
            side_hop(s - SLAG - YLAG, got_ys)

        return 0

    def grad_part(col):
        copy(sb.at[col, :, oc], sb.at[col, :, oc], cs_s, cs_r.at[col], here).wait_recv()
        for k in (2, 1, 3, 0):
            z0 = (m % 4 + k) % 4
            to = 4 * col + z0
            block = sb[col, pl.ds(4 * z0, 4)].reshape(1024, 128)
            snd_g[to] = jnp.dot(grads[...], block, preferred_element_type=F32).astype(BF16)

            @pl.when(to != m)
            def _():
                copy(snd_g.at[to], rcv_g.at[m], xg_s, xg_r, {"dp": d, "mp": to}).start()

            @pl.when(to == m)
            def _():
                rcv_g[m] = snd_g[to]

    def act_part(off, piece, width):
        lhs = piece[...].reshape(NZ * 40, width)
        return lax.dot_general(
            lhs, acts[:, off:off + width], (((1,), (1,)), ((), ())), preferred_element_type=F32
        )

    def act_first():
        get_a.wait()
        copy(ga.at[oc], ga.at[oc], ca_s, ca_r, here).wait_recv()
        acc[...] = act_part(0, ga.at[0, 0], 256)
        for cc in range(2):
            for q in range(NC):
                if cc or q:
                    acc[...] += act_part(cc * HALF + 256 * q, ga.at[cc, q], 256)

    def act_rest():
        copy(gb.at[oc], gb.at[oc], cb_s, cb_r, here).wait_recv()
        for cc in range(2):
            for yy in range(2):
                acc[...] += act_part(cc * HALF + NA + yy * NB, gb.at[cc, yy], NB)
        for mm in range(NM):
            yy, z0 = mm // 4, 4 * (mm % 4)
            for i in range(4):
                src = 40 * (z0 + i) + 20 * yy
                mix[20 * i:20 * (i + 1), :256] = acc[src:src + 20, :]
            snd_a[mm] = mix[:KM, :256].astype(BF16)
        for t in range(1, NM):
            to = (m + t) % NM
            copy(snd_a.at[to], rcv_a.at[m], xa_s, xa_r, {"dp": d, "mp": to}).start()
        rcv_a[m] = snd_a[m]


    lax.fori_loop(1, 9, step, 0)
    act_first()
    lax.fori_loop(9, 9 + SLAG, step, 0)
    get_g.wait()
    grad_part(y)
    lax.fori_loop(9 + SLAG, 9 + YLAG, step, 0)
    act_rest()
    lax.fori_loop(9 + YLAG, 9 + SLAG + YLAG, step, 0)
    grad_part(oy)

    copy(rcv_g.at[:7], rcv_g.at[:7], xg_s, xg_r, here).wait_recv()
    total = rcv_g[0].astype(F32)
    for s in range(1, NM):
        total += rcv_g[s].astype(F32)
    g_t = total.T.astype(BF16)
    for i in range(8):
        own_g[i % 2, 16 * (i // 2):16 * (i // 2 + 1), :] = g_t[16 * i:16 * (i + 1), :]
    mine_g = c * NM + m
    for t in range(1, NM):
        to = (m + t) % NM
        copy(own_g.at[c], gt.at[mine_g], gt_s, gt_r, {"dp": d, "mp": to}).start()
        copy(own_g.at[oc], gt.at[mine_g], gt_s, gt_r, {"dp": d_other, "mp": to}).start()
    copy(own_g.at[oc], gt.at[mine_g], gt_s, gt_r, core).start()
    gt[mine_g] = own_g[c]
    copy(rcv_a.at[:7], rcv_a.at[:7], xa_s, xa_r, here).wait_recv()
    total = rcv_a[0].astype(F32)
    for s in range(1, NM):
        total += rcv_a[s].astype(F32)
    act[c, :KM, :] = total.astype(BF16)
    copy(act.at[c, :KM], act.at[c, :KM], ac_s, ac_r, core).start()
    copy(act.at[oc, :KM], act.at[oc, :KM], ac_s, ac_r, here).wait_recv()

    copy(gt.at[:15], gt.at[:15], gt_s, gt_r, here).wait_recv()

    nt = (((1,), (1,)), ((), ()))
    groups = [(z // 4 + q) % 4 for q in (2, 1, 3, 0)]
    for half in (oy, y):
        rot = jnp.zeros((256, 128), F32)
        sq = jnp.zeros((256, 128), F32)
        for cc in range(2):
            a_val = act[cc]
            g_val = gt[pl.ds(cc * NM + 4 * half, 4)].reshape(256, 256)
            rot += lax.dot_general(g_val, a_val, nt, preferred_element_type=F32)
            a_sq = (a_val.astype(F32) ** 2).astype(BF16)
            g_sq = (g_val.astype(F32) ** 2).astype(BF16)
            sq += lax.dot_general(g_sq, a_sq, nt, preferred_element_type=F32)
        part[half, :, 0] = rot.astype(BF16).reshape(NZ, 16, 128)
        part[half, :, 1] = sq.astype(BF16).reshape(NZ, 16, 128)
        if half is oy:
            for q, g in enumerate(groups):
                mine = pl.ds(4 * g, 4)
                copy(part.at[oy, mine], r1.at[mine], p1_s, p1_r.at[q], yside).start()
    for q, g in enumerate(groups):
        mine = pl.ds(4 * g, 4)
        copy(r1.at[:4], r1.at[:4], p1_s, p1_r.at[q], here).wait_recv()
        p2[mine] = (part[y, mine].astype(F32) + r1[mine].astype(F32)).astype(BF16)
        for i in range(4):
            to = 4 * g + i

            @pl.when(to != z)
            def _():
                copy(p2.at[to], r2.at[z], p2_s, p2_r, dev(y, to, c)).start()
    r2[z] = p2[z]
    copy(r2.at[:15], r2.at[:15], p2_s, p2_r, here).wait_recv()
    total = r2[0].astype(F32)
    for s in range(1, NZ):
        total += r2[s].astype(F32)
    diag = total[1] / tokens_all
    diag_t[...] = diag[:, :KM]
    sc[y, z, c] = (total[0] / (diag + damping[0])).astype(BF16)

    for t in range(1, NZ):
        copy(sc.at[y, z, c], sc.at[y, z, c], sz_s, sz_r.at[z // 4], dev(y, (z + t) % NZ, c)).start()
    groups = [(z // 4 + q) % 4 for q in (0, 1, 3, 2)]
    for q, g in enumerate(groups):
        mine = pl.ds(4 * g, 4)
        width = 4 if q else 3
        copy(sc.at[0, :width, 0], sc.at[0, :width, 0], sz_s, sz_r.at[g], here).wait_recv()
        for yy, cc in quad:
            copy(sc.at[y, mine, c], sc.at[y, mine, c], sq_s, sq_r, dev(yy, z, cc)).start()
    own_o.wait()
    copy(bo.at[:7], bo.at[:7], bo_s, bo_r, here).wait_recv()
    copy(sc.at[:, :12], sc.at[:, :12], sq_s, sq_r, here).wait_recv()

    total = jnp.zeros((128, 128), F32)
    for mm in range(NM):
        yy, z0 = mm // 4, 4 * (mm % 4)
        total += jnp.dot(bo[mm], sc[yy, z0:z0 + 4].reshape(128, 128), preferred_element_type=F32)
    bk[m] = total.T[:KM, :].astype(BF16)
    for t in range(1, NM):
        copy(bk.at[m], bk.at[m], bk_s, bk_r, {"dp": d, "mp": (m + t) % NM}).start()
    copy(bk.at[:7], bk.at[:7], bk_s, bk_r, here).wait_recv()
    for mm in range(NM):
        yy, z0 = mm // 4, 4 * (mm % 4)
        b_val = bk[mm].astype(F32)
        for i in range(4):
            dst = 40 * (z0 + i) + 20 * yy
            bf[dst:dst + 20, :] = b_val[20 * i:20 * (i + 1), :]
    back_t = bf[...].T.astype(BF16)
    for cc in range(2):
        for off, piece, width in (
            *((cc * HALF + 256 * q, ga.at[cc, q], 256) for q in range(NC)),
            (cc * HALF + NA, gb.at[cc, 0], NB),
            (cc * HALF + NA + NB, gb.at[cc, 1], NB),
        ):
            rhs = piece[...].reshape(NZ * 40, width)
            up = jnp.dot(back_t, rhs, preferred_element_type=F32)
            update[off:off + width, :] = up.T.astype(BF16)

    @pl.when(far)
    def _():
        copy(bout, bout, sw_s, sw_r, here).wait_send()

    def sent(ref, ssem):
        copy(ref, ref, ssem, sw_r, here).wait_send()

    sent(qa.at[:3], q_s.at[0])
    sent(qb.at[:3], q_s.at[1])
    sent(bo.at[:7], bo_s)
    sent(snd_a.at[:7], xa_s)
    sent(snd_g.at[:7], xg_s)
    sent(gt.at[:15], gt_s)
    sent(act.at[0, :KM], ac_s)
    sent(bk.at[:7], bk_s)
    sent(r1, p1_s)
    sent(p2.at[:15], p2_s)
    sent(sc.at[0, :15, 0], sz_s)
    sent(sc.at[:, :12], sq_s)
    sent(ga.at[0, :, :15], ra_s)
    sent(gb.at[0, 0, :15], rb_s)
    sent(sb.at[0, :15, 0], rs_s)
    sent(gb.at[0, 0], yb_s)
    sent(sb.at[0, :, 0], ys_s)
    sent(ga.at[0], ca_s)
    sent(gb.at[0], cb_s)
    sent(sb.at[:, :, 0], cs_s)


def solution(mesh):
    def on_device(acts, grads, basis_in, basis_out, damping):
        tokens_all = acts.shape[0] * mesh.shape["dp"]
        vmem = pl.BlockSpec(memory_space=pltpu.VMEM)
        dma = pltpu.SemaphoreType.DMA
        v = pltpu.VMEM

        def hbm(array):
            return pltpu.with_memory_space_constraint(array, pltpu.MemorySpace.HBM)

        def body(*refs):
            kernel(tokens_all, *refs)

        update, diag_t = pl.pallas_call(
            body,
            out_shape=(
                jax.ShapeDtypeStruct((3584, 128), BF16),
                jax.ShapeDtypeStruct((16, KM), F32),
            ),
            in_specs=[pl.BlockSpec(memory_space=pltpu.MemorySpace.HBM)] * 4 + [pl.BlockSpec(memory_space=pltpu.SMEM)],
            out_specs=(vmem, vmem),
            scratch_shapes=[
                v(acts.shape, BF16), v(grads.shape, BF16),
                v((NQ, KD, NA), BF16), v((NQ, KD, NB), BF16), v((KM, NA + NB), F32),
                v((2, NC, NZ, 40, 256), BF16), v((2, 2, NZ, 40, NB), BF16),
                v((2, NZ, 2, 128, 128), BF16), v((NM, 128, 128), BF16), v((640, 256), F32),
                v((NM, KM, 256), BF16), v((NM, 256, 128), BF16),
                v((NM, KM, 256), BF16), v((NM, 256, 128), BF16),
                v((2, 128, 256), BF16), v((2, 64, 256), BF16), v((2 * NM, 64, 256), BF16),
                v((2, NZ, 2, 16, 128), BF16), v((NZ, 2, 16, 128), BF16),
                v((NZ, 2, 16, 128), BF16), v((NZ, 2, 16, 128), BF16),
                v((2, NZ, 2, 16, 128), BF16), v((NM, KM, 128), BF16), v((640, 128), F32),
                dma((2,)), dma((2,)), dma, dma((NC, NZ)), dma, dma((NZ,)), dma, dma((NZ,)),
                dma, dma((NZ,)), dma, dma((NZ,)),
                dma, dma, dma, dma, dma, dma((2,)), dma, dma, dma, dma,
                dma, dma, dma, dma, dma, dma,
                dma, dma((4,)), dma, dma,
                dma, dma((4,)), dma, dma, dma, dma, dma((6,)), dma, dma,
            ],
            compiler_params=pltpu.CompilerParams(
                collective_id=0, has_side_effects=True, vmem_limit_bytes=40 * 2**20
            ),
        )(hbm(acts), hbm(grads), hbm(basis_in.T), hbm(basis_out), damping)
        return update, diag_t.T

    placed = (P("dp", "mp"), P("dp", "mp"), P("mp", "dp"), P("dp", "mp"), P())
    return jax.shard_map(
        on_device,
        mesh=mesh,
        in_specs=placed,
        out_specs=(P("mp", "dp"), P("mp", "dp")),
        check_vma=False,
    )
```

```python
import jax
import jax.numpy as jnp
from jax import lax
from jax.experimental import pallas as pl
from jax.experimental.pallas import tpu as pltpu
from jax.sharding import PartitionSpec as P

F32 = jnp.float32
BF16 = jnp.bfloat16
MESH = pl.DeviceIdType.MESH

NZ = 16
NQ = 4
NM = 8
KD = 10
KM = 80
NA = 1024
NB = 384
HALF = NA + 2 * NB
NC = 4
YLAG = 2


def kernel(
    tokens_all,
    acts_h, grads_h, bin_t, bout, damping,
    update, diag_t,
    acts, grads, bin_v,
    qa, qb, mix, ga, gb, sb, bo, bt, acc,
    snd_a, snd_g, rcv_a, rcv_g, act, own_g, gt, part, r1, p2, r2, sc, bk, bf,
    q_s, q_r, ra_s, ra_r, rb_s, rb_r, yb_s, yb_r, rs_s, rs_r, ys_s, ys_r,
    ca_s, ca_r, cb_s, cb_r, cs_s, cs_r, sw_s, sw_r, bo_s, bo_r,
    xa_s, xa_r, xg_s, xg_r, gt_s, gt_r, p1_s, p1_r, p2_s, p2_r,
    sz_s, sz_r, sq_s, sq_r, bk_s, bk_r, in_s, ac_s, ac_r,
):
    d = lax.axis_index("dp")
    m = lax.axis_index("mp")
    y = d // 32
    z = (d // 2) % 16
    c = d % 2
    oy = 1 - y
    oc = 1 - c
    me_q = 2 * y + c
    d_other = d + 1 - 2 * c

    def dev(yy, zz, cc):
        return {"dp": yy * 32 + zz * 2 + cc, "mp": m}

    def copy(src, dst, ssem, rsem, device):
        return pltpu.make_async_remote_copy(
            src_ref=src, dst_ref=dst, send_sem=ssem, recv_sem=rsem,
            device_id=device, device_id_type=MESH,
        )

    here = {"dp": d, "mp": m}
    right = dev(y, (z + 1) % NZ, c)
    left = dev(y, (z + NZ - 1) % NZ, c)
    core = dev(y, z, oc)
    yside = dev(oy, z, c)
    quad = [(y, oc), (oy, c), (oy, oc)]
    swap_a = d // 8
    swap_d = 8 * m + d % 8
    far = swap_a != m

    act[:, KM:, :] = jnp.zeros((2, 128 - KM, 256), BF16)
    barrier = pltpu.get_barrier_semaphore()

    def greet(device):
        pl.semaphore_signal(barrier, inc=1, device_id=device, device_id_type=MESH)

    for t in range(1, NZ):
        greet(dev(y, (z + t) % NZ, c))
    for yy, cc in quad:
        greet(dev(yy, z, cc))
    for t in range(1, NM):
        greet({"dp": d, "mp": (m + t) % NM})
        greet({"dp": d_other, "mp": (m + t) % NM})

    @pl.when(far)
    def _():
        greet({"dp": swap_d, "mp": swap_a})

    a_off = pl.multiple_of(c * HALF, 128)
    b_off = pl.multiple_of(c * HALF + NA + y * NB, 128)
    get_b = pltpu.make_async_copy(bin_t, bin_v, in_s.at[0])
    own_o = pltpu.make_async_copy(bout, bo.at[m], in_s.at[2])
    get_g = pltpu.make_async_copy(grads_h, grads, in_s.at[4])
    get_a = pltpu.make_async_copy(acts_h, acts, in_s.at[5])
    own_o.start()
    get_b.start()

    get_g.start()
    get_a.start()
    own_o.wait()
    bt[...] = bo[m].astype(F32).T.astype(BF16)
    get_b.wait()
    qa[me_q] = bin_v[:, pl.ds(a_off, NA)]
    qb[me_q] = bin_v[:, pl.ds(b_off, NB)]

    @pl.when(jnp.logical_not(far))
    def _():
        sb[y, z, c] = bt[...]

    pl.semaphore_wait(barrier, NZ - 1 + 3 + 2 * (NM - 1) + far.astype(jnp.int32))

    @pl.when(far)
    def _():
        copy(bt, sb.at[swap_d // 32, (swap_d // 2) % 16, swap_d % 2], sw_s, sw_r,
             {"dp": swap_d, "mp": swap_a}).start()

    for yy, cc in quad:
        a_to = pl.multiple_of(cc * HALF, 128)
        b_to = pl.multiple_of(cc * HALF + NA + yy * NB, 128)
        copy(bin_v.at[:, pl.ds(a_to, NA)], qa.at[me_q], q_s.at[0], q_r.at[0], dev(yy, z, cc)).start()
        copy(bin_v.at[:, pl.ds(b_to, NB)], qb.at[me_q], q_s.at[1], q_r.at[1], dev(yy, z, cc)).start()
    for t in range(1, NM):
        copy(bout, bo.at[m], bo_s, bo_r, {"dp": d, "mp": (m + t) % NM}).start()

    def ring_a(q):
        def send(zz, device):
            copy(ga.at[c, q, zz], ga.at[c, q, zz], ra_s, ra_r.at[q, zz], device).start()

        return send

    def ring_b(zz, device):
        copy(gb.at[c, y, zz], gb.at[c, y, zz], rb_s, rb_r.at[zz], device).start()

    def ring_s(zz, device):
        copy(sb.at[y, zz, c], sb.at[y, zz, c], rs_s, rs_r.at[zz], device).start()

    def side_b(zz):
        copy(gb.at[c, y, zz], gb.at[c, y, zz], yb_s, yb_r.at[zz], yside).start()
        core_b(y, zz)

    def side_s(zz):
        copy(sb.at[y, zz, c], sb.at[y, zz, c], ys_s, ys_r.at[zz], yside).start()
        core_s(y, zz)

    def core_a(q):
        def send(zz):
            copy(ga.at[c, q, zz], ga.at[c, q, zz], ca_s, ca_r, core).start()

        return send

    def core_b(yy, zz):
        copy(gb.at[c, yy, zz], gb.at[c, yy, zz], cb_s, cb_r, core).start()

    def core_s(yy, zz):
        copy(sb.at[yy, zz, c], sb.at[yy, zz, c], cs_s, cs_r.at[yy], core).start()

    def got_a(q):
        def wait(zz):
            copy(ga.at[c, q, zz], ga.at[c, q, zz], ra_s, ra_r.at[q, zz], here).wait_recv()

        return wait

    def got_b(zz):
        copy(gb.at[c, y, zz], gb.at[c, y, zz], rb_s, rb_r.at[zz], here).wait_recv()

    def got_s(zz):
        copy(sb.at[y, zz, c], sb.at[y, zz, c], rs_s, rs_r.at[zz], here).wait_recv()

    def got_yb(zz):
        copy(gb.at[c, oy, zz], gb.at[c, oy, zz], yb_s, yb_r.at[zz], here).wait_recv()
        core_b(oy, zz)

    def got_ys(zz):
        copy(sb.at[oy, zz, c], sb.at[oy, zz, c], ys_s, ys_r.at[zz], here).wait_recv()
        core_s(oy, zz)

    copy(qa.at[:3], qa.at[:3], q_s.at[0], q_r.at[0], here).wait_recv()
    copy(qb.at[:3], qb.at[:3], q_s.at[1], q_r.at[1], here).wait_recv()
    for s in range(NQ):
        mix[KD * s:KD * (s + 1), :NA] = qa[s].astype(F32)
        mix[KD * s:KD * (s + 1), NA:] = qb[s].astype(F32)
    for q in range(NC):
        ga[c, q, z] = mix[:40, 256 * q:256 * (q + 1)].astype(BF16)
    gb[c, y, z] = mix[:40, NA:].astype(BF16)

    for q in range(NC):
        ring_a(q)(z, right)
        ring_a(q)(z, left)
        core_a(q)(z)
    ring_b(z, right)
    ring_b(z, left)
    side_b(z)

    @pl.when(far)
    def _():
        copy(sb.at[y, z, c], sb.at[y, z, c], sw_s, sw_r, here).wait_recv()

    ring_s(z, right)
    ring_s(z, left)
    side_s(z)

    def hop(t, got, ring, side, last):
        zr = (z - t + NZ) % NZ
        zl = (z + t) % NZ
        for zz, device, reach in ((zr, right, 8 if last == 0 else 7), (zl, left, 8 if last == 1 else 7)):
            @pl.when(t <= reach)
            def _():
                got(zz)

                @pl.when(t < reach)
                def _():
                    ring(zz, device)

                side(zz)

    def side_hop(t, got):
        got((z - t + NZ) % NZ)

        @pl.when((t > 0) & (t < 8))
        def _():
            got((z + t) % NZ)

    def step(s, _):
        @pl.when(s <= 8)
        def _():
            for q in range(NC):
                hop(s, got_a(q), ring_a(q), core_a(q), q % 2)
            hop(s, got_b, ring_b, side_b, 0)
            hop(s, got_s, ring_s, side_s, 1)

        @pl.when(s >= YLAG)
        def _():
            side_hop(s - YLAG, got_yb)
            side_hop(s - YLAG, got_ys)

        return 0

    def grad_part(col):
        copy(sb.at[col, :, oc], sb.at[col, :, oc], cs_s, cs_r.at[col], here).wait_recv()
        prod = None
        for zz in range(4):
            lhs = jnp.concatenate(
                [jnp.concatenate([sb[col, 4 * b + zz, cc] for b in range(4)], axis=0) for cc in range(2)], axis=1
            )
            term = lax.dot_general(
                lhs, grads[:, 256 * zz:256 * (zz + 1)], (((1,), (1,)), ((), ())), preferred_element_type=F32
            )
            prod = term if prod is None else prod + term
        for b in range(4):
            snd_g[4 * col + b] = prod[128 * b:128 * (b + 1), :].astype(BF16)
        for k in (2, 1, 3, 0):
            to = 4 * col + (m % 4 + k) % 4

            @pl.when(to != m)
            def _():
                copy(snd_g.at[to], rcv_g.at[m], xg_s, xg_r, {"dp": d, "mp": to}).start()

            @pl.when(to == m)
            def _():
                rcv_g[m] = snd_g[to]

    def act_part(off, piece, width):
        lhs = piece[...].reshape(NZ * 40, width)
        return lax.dot_general(
            lhs, acts[:, off:off + width], (((1,), (1,)), ((), ())), preferred_element_type=F32
        )

    def act_first():
        get_a.wait()
        copy(ga.at[oc], ga.at[oc], ca_s, ca_r, here).wait_recv()
        acc[...] = act_part(0, ga.at[0, 0], 256)
        for cc in range(2):
            for q in range(NC):
                if cc or q:
                    acc[...] += act_part(cc * HALF + 256 * q, ga.at[cc, q], 256)

    def act_rest():
        copy(gb.at[oc], gb.at[oc], cb_s, cb_r, here).wait_recv()
        for cc in range(2):
            for yy in range(2):
                acc[...] += act_part(cc * HALF + NA + yy * NB, gb.at[cc, yy], NB)
        for mm in range(NM):
            yy, z0 = mm // 4, 4 * (mm % 4)
            for i in range(4):
                src = 40 * (z0 + i) + 20 * yy
                mix[20 * i:20 * (i + 1), :256] = acc[src:src + 20, :]
            snd_a[mm] = mix[:KM, :256].astype(BF16)
        for t in range(1, NM):
            to = (m + t) % NM
            copy(snd_a.at[to], rcv_a.at[m], xa_s, xa_r, {"dp": d, "mp": to}).start()
        rcv_a[m] = snd_a[m]


    lax.fori_loop(1, 9, step, 0)
    act_first()
    lax.fori_loop(9, 9 + YLAG, step, 0)
    get_g.wait()
    grad_part(1 - m // 4)
    grad_part(m // 4)
    act_rest()

    copy(rcv_g.at[:7], rcv_g.at[:7], xg_s, xg_r, here).wait_recv()
    total = rcv_g[0].astype(F32)
    for s in range(1, NM):
        total += rcv_g[s].astype(F32)
    g_t = total.astype(BF16)
    for i in range(8):
        own_g[i % 2, 16 * (i // 2):16 * (i // 2 + 1), :] = g_t[16 * i:16 * (i + 1), :]
    mine_g = c * NM + m
    for t in range(1, NM):
        to = (m + t) % NM
        copy(own_g.at[c], gt.at[mine_g], gt_s, gt_r, {"dp": d, "mp": to}).start()
        copy(own_g.at[oc], gt.at[mine_g], gt_s, gt_r, {"dp": d_other, "mp": to}).start()
    copy(own_g.at[oc], gt.at[mine_g], gt_s, gt_r, core).start()
    gt[mine_g] = own_g[c]
    copy(rcv_a.at[:7], rcv_a.at[:7], xa_s, xa_r, here).wait_recv()
    total = rcv_a[0].astype(F32)
    for s in range(1, NM):
        total += rcv_a[s].astype(F32)
    act[c, :KM, :] = total.astype(BF16)
    copy(act.at[c, :KM], act.at[c, :KM], ac_s, ac_r, core).start()
    copy(act.at[oc, :KM], act.at[oc, :KM], ac_s, ac_r, here).wait_recv()

    copy(gt.at[:15], gt.at[:15], gt_s, gt_r, here).wait_recv()

    nt = (((1,), (1,)), ((), ()))
    groups = [(z // 4 + q) % 4 for q in (2, 1, 3, 0)]
    for half in (oy, y):
        rot = jnp.zeros((256, 128), F32)
        sq = jnp.zeros((256, 128), F32)
        for cc in range(2):
            a_val = act[cc]
            g_val = gt[pl.ds(cc * NM + 4 * half, 4)].reshape(256, 256)
            rot += lax.dot_general(g_val, a_val, nt, preferred_element_type=F32)
            a_sq = (a_val.astype(F32) ** 2).astype(BF16)
            g_sq = (g_val.astype(F32) ** 2).astype(BF16)
            sq += lax.dot_general(g_sq, a_sq, nt, preferred_element_type=F32)
        part[half, :, 0] = rot.astype(BF16).reshape(NZ, 16, 128)
        part[half, :, 1] = sq.astype(BF16).reshape(NZ, 16, 128)
        if half is oy:
            for q, g in enumerate(groups):
                mine = pl.ds(4 * g, 4)
                copy(part.at[oy, mine], r1.at[mine], p1_s, p1_r.at[q], yside).start()
    for q, g in enumerate(groups):
        mine = pl.ds(4 * g, 4)
        copy(r1.at[:4], r1.at[:4], p1_s, p1_r.at[q], here).wait_recv()
        p2[mine] = (part[y, mine].astype(F32) + r1[mine].astype(F32)).astype(BF16)
        for i in range(4):
            to = 4 * g + i

            @pl.when(to != z)
            def _():
                copy(p2.at[to], r2.at[z], p2_s, p2_r, dev(y, to, c)).start()
    r2[z] = p2[z]
    copy(r2.at[:15], r2.at[:15], p2_s, p2_r, here).wait_recv()
    total = r2[0].astype(F32)
    for s in range(1, NZ):
        total += r2[s].astype(F32)
    diag = total[1] / tokens_all
    diag_t[...] = diag[:, :KM]
    sc[y, z, c] = (total[0] / (diag + damping[0])).astype(BF16)

    for t in range(1, NZ):
        copy(sc.at[y, z, c], sc.at[y, z, c], sz_s, sz_r.at[z // 4], dev(y, (z + t) % NZ, c)).start()
    groups = [(z // 4 + q) % 4 for q in (0, 1, 3, 2)]
    for q, g in enumerate(groups):
        mine = pl.ds(4 * g, 4)
        width = 4 if q else 3
        copy(sc.at[0, :width, 0], sc.at[0, :width, 0], sz_s, sz_r.at[g], here).wait_recv()
        for yy, cc in quad:
            copy(sc.at[y, mine, c], sc.at[y, mine, c], sq_s, sq_r, dev(yy, z, cc)).start()
    copy(bo.at[:7], bo.at[:7], bo_s, bo_r, here).wait_recv()
    copy(sc.at[:, :12], sc.at[:, :12], sq_s, sq_r, here).wait_recv()

    total = jnp.zeros((128, 128), F32)
    for mm in range(NM):
        yy, z0 = mm // 4, 4 * (mm % 4)
        total += jnp.dot(bo[mm], sc[yy, z0:z0 + 4].reshape(128, 128), preferred_element_type=F32)
    bk[m] = total.T[:KM, :].astype(BF16)
    for t in range(1, NM):
        copy(bk.at[m], bk.at[m], bk_s, bk_r, {"dp": d, "mp": (m + t) % NM}).start()
    copy(bk.at[:7], bk.at[:7], bk_s, bk_r, here).wait_recv()
    for mm in range(NM):
        yy, z0 = mm // 4, 4 * (mm % 4)
        b_val = bk[mm].astype(F32)
        for i in range(4):
            dst = 40 * (z0 + i) + 20 * yy
            bf[dst:dst + 20, :] = b_val[20 * i:20 * (i + 1), :]
    back_t = bf[...].T.astype(BF16)
    for cc in range(2):
        for off, piece, width in (
            *((cc * HALF + 256 * q, ga.at[cc, q], 256) for q in range(NC)),
            (cc * HALF + NA, gb.at[cc, 0], NB),
            (cc * HALF + NA + NB, gb.at[cc, 1], NB),
        ):
            rhs = piece[...].reshape(NZ * 40, width)
            up = jnp.dot(back_t, rhs, preferred_element_type=F32)
            update[off:off + width, :] = up.T.astype(BF16)

    @pl.when(far)
    def _():
        copy(bt, bt, sw_s, sw_r, here).wait_send()

    def sent(ref, ssem):
        copy(ref, ref, ssem, sw_r, here).wait_send()

    sent(qa.at[:3], q_s.at[0])
    sent(qb.at[:3], q_s.at[1])
    sent(bo.at[:7], bo_s)
    sent(snd_a.at[:7], xa_s)
    sent(snd_g.at[:7], xg_s)
    sent(gt.at[:15], gt_s)
    sent(act.at[0, :KM], ac_s)
    sent(bk.at[:7], bk_s)
    sent(r1, p1_s)
    sent(p2.at[:15], p2_s)
    sent(sc.at[0, :15, 0], sz_s)
    sent(sc.at[:, :12], sq_s)
    sent(ga.at[0, :, :15], ra_s)
    sent(gb.at[0, 0, :15], rb_s)
    sent(sb.at[0, :15, 0], rs_s)
    sent(gb.at[0, 0], yb_s)
    sent(sb.at[0, :, 0], ys_s)
    sent(ga.at[0], ca_s)
    sent(gb.at[0], cb_s)
    sent(sb.at[:, :, 0], cs_s)


def solution(mesh):
    def on_device(acts, grads, basis_in, basis_out, damping):
        tokens_all = acts.shape[0] * mesh.shape["dp"]
        vmem = pl.BlockSpec(memory_space=pltpu.VMEM)
        dma = pltpu.SemaphoreType.DMA
        v = pltpu.VMEM

        def hbm(array):
            return pltpu.with_memory_space_constraint(array, pltpu.MemorySpace.HBM)

        def body(*refs):
            kernel(tokens_all, *refs)

        update, diag_t = pl.pallas_call(
            body,
            out_shape=(
                jax.ShapeDtypeStruct((3584, 128), BF16),
                jax.ShapeDtypeStruct((16, KM), F32),
            ),
            in_specs=[pl.BlockSpec(memory_space=pltpu.MemorySpace.HBM)] * 4 + [pl.BlockSpec(memory_space=pltpu.SMEM)],
            out_specs=(vmem, vmem),
            scratch_shapes=[
                v(acts.shape, BF16), v(grads.shape, BF16), v((KD, acts.shape[1]), BF16),
                v((NQ, KD, NA), BF16), v((NQ, KD, NB), BF16), v((KM, NA + NB), F32),
                v((2, NC, NZ, 40, 256), BF16), v((2, 2, NZ, 40, NB), BF16),
                v((2, NZ, 2, 128, 128), BF16), v((NM, 128, 128), BF16), v((128, 128), BF16), v((640, 256), F32),
                v((NM, KM, 256), BF16), v((NM, 128, 256), BF16),
                v((NM, KM, 256), BF16), v((NM, 128, 256), BF16),
                v((2, 128, 256), BF16), v((2, 64, 256), BF16), v((2 * NM, 64, 256), BF16),
                v((2, NZ, 2, 16, 128), BF16), v((NZ, 2, 16, 128), BF16),
                v((NZ, 2, 16, 128), BF16), v((NZ, 2, 16, 128), BF16),
                v((2, NZ, 2, 16, 128), BF16), v((NM, KM, 128), BF16), v((640, 128), F32),
                dma((2,)), dma((2,)), dma, dma((NC, NZ)), dma, dma((NZ,)), dma, dma((NZ,)),
                dma, dma((NZ,)), dma, dma((NZ,)),
                dma, dma, dma, dma, dma, dma((2,)), dma, dma, dma, dma,
                dma, dma, dma, dma, dma, dma,
                dma, dma((4,)), dma, dma,
                dma, dma((4,)), dma, dma, dma, dma, dma((6,)), dma, dma,
            ],
            compiler_params=pltpu.CompilerParams(
                collective_id=0, has_side_effects=True, vmem_limit_bytes=40 * 2**20
            ),
        )(hbm(acts), hbm(grads), hbm(basis_in.T), hbm(basis_out), damping)
        return update, diag_t.T

    placed = (P("dp", "mp"), P("dp", "mp"), P("mp", "dp"), P("dp", "mp"), P())
    return jax.shard_map(
        on_device,
        mesh=mesh,
        in_specs=placed,
        out_specs=(P("mp", "dp"), P("mp", "dp")),
        check_vma=False,
    )
```

```python
import jax
import jax.numpy as jnp
from jax import lax
from jax.experimental import pallas as pl
from jax.experimental.pallas import tpu as pltpu
from jax.sharding import PartitionSpec as P

F32 = jnp.float32
BF16 = jnp.bfloat16
MESH = pl.DeviceIdType.MESH

NZ = 16
NQ = 4
NM = 8
KD = 10
KM = 80
NA = 1024
NB = 384
HALF = NA + 2 * NB
NC = 4
YLAG = 2


def kernel(
    tokens_all,
    acts_h, grads_h, bin_t, bout, damping,
    update, diag_t,
    acts, grads, bin_v,
    qa, qb, mix, ga, gb, sb, bo, bt, acc,
    snd_a, snd_g, rcv_a, rcv_g, act, own_g, gt, part, r1, p2, r2, sc, bk, bf,
    q_s, q_r, ra_s, ra_r, rb_s, rb_r, yb_s, yb_r, rs_s, rs_r, ys_s, ys_r,
    ca_s, ca_r, cb_s, cb_r, cs_s, cs_r, sw_s, sw_r, bo_s, bo_r,
    xa_s, xa_r, xg_s, xg_r, gt_s, gt_r, p1_s, p1_r, p2_s, p2_r,
    sz_s, sz_r, sq_s, sq_r, bk_s, bk_r, in_s, ac_s, ac_r,
):
    d = lax.axis_index("dp")
    m = lax.axis_index("mp")
    y = d // 32
    z = (d // 2) % 16
    c = d % 2
    oy = 1 - y
    oc = 1 - c
    me_q = 2 * y + c
    d_other = d + 1 - 2 * c

    def dev(yy, zz, cc):
        return {"dp": yy * 32 + zz * 2 + cc, "mp": m}

    def copy(src, dst, ssem, rsem, device):
        return pltpu.make_async_remote_copy(
            src_ref=src, dst_ref=dst, send_sem=ssem, recv_sem=rsem,
            device_id=device, device_id_type=MESH,
        )

    here = {"dp": d, "mp": m}
    right = dev(y, (z + 1) % NZ, c)
    left = dev(y, (z + NZ - 1) % NZ, c)
    core = dev(y, z, oc)
    yside = dev(oy, z, c)
    quad = [(y, oc), (oy, c), (oy, oc)]
    swap_a = d // 8
    swap_d = 8 * m + d % 8
    far = swap_a != m

    act[:, KM:, :] = jnp.zeros((2, 128 - KM, 256), BF16)
    barrier = pltpu.get_barrier_semaphore()

    def greet(device):
        pl.semaphore_signal(barrier, inc=1, device_id=device, device_id_type=MESH)

    for t in range(1, NZ):
        greet(dev(y, (z + t) % NZ, c))
    for yy, cc in quad:
        greet(dev(yy, z, cc))
    for t in range(1, NM):
        greet({"dp": d, "mp": (m + t) % NM})
        greet({"dp": d_other, "mp": (m + t) % NM})

    @pl.when(far)
    def _():
        greet({"dp": swap_d, "mp": swap_a})

    a_off = pl.multiple_of(c * HALF, 128)
    b_off = pl.multiple_of(c * HALF + NA + y * NB, 128)
    get_b = pltpu.make_async_copy(bin_t, bin_v, in_s.at[0])
    own_o = pltpu.make_async_copy(bout, bo.at[m], in_s.at[2])
    get_g = pltpu.make_async_copy(grads_h, grads, in_s.at[4])
    get_a = pltpu.make_async_copy(acts_h, acts, in_s.at[5])
    own_o.start()
    get_b.start()

    get_g.start()
    get_a.start()
    own_o.wait()
    bt[...] = bo[m].astype(F32).T.astype(BF16)
    get_b.wait()
    qa[me_q] = bin_v[:, pl.ds(a_off, NA)]
    qb[me_q] = bin_v[:, pl.ds(b_off, NB)]

    @pl.when(jnp.logical_not(far))
    def _():
        sb[y, z, c] = bt[...]

    pl.semaphore_wait(barrier, NZ - 1 + 3 + 2 * (NM - 1) + far.astype(jnp.int32))

    @pl.when(far)
    def _():
        copy(bt, sb.at[swap_d // 32, (swap_d // 2) % 16, swap_d % 2], sw_s, sw_r,
             {"dp": swap_d, "mp": swap_a}).start()

    for yy, cc in quad:
        a_to = pl.multiple_of(cc * HALF, 128)
        b_to = pl.multiple_of(cc * HALF + NA + yy * NB, 128)
        copy(bin_v.at[:, pl.ds(a_to, NA)], qa.at[me_q], q_s.at[0], q_r.at[0], dev(yy, z, cc)).start()
        copy(bin_v.at[:, pl.ds(b_to, NB)], qb.at[me_q], q_s.at[1], q_r.at[1], dev(yy, z, cc)).start()
    for t in range(1, NM):
        copy(bout, bo.at[m], bo_s, bo_r, {"dp": d, "mp": (m + t) % NM}).start()

    def ring_a(q):
        def send(zz, device):
            copy(ga.at[c, q, zz], ga.at[c, q, zz], ra_s, ra_r.at[q, zz], device).start()

        return send

    def ring_b(zz, device):
        copy(gb.at[c, y, zz], gb.at[c, y, zz], rb_s, rb_r.at[zz], device).start()

    def ring_s(zz, device):
        copy(sb.at[y, zz, c], sb.at[y, zz, c], rs_s, rs_r.at[zz], device).start()

    def side_b(zz):
        copy(gb.at[c, y, zz], gb.at[c, y, zz], yb_s, yb_r.at[zz], yside).start()
        core_b(y, zz)

    def side_s(zz):
        copy(sb.at[y, zz, c], sb.at[y, zz, c], ys_s, ys_r.at[zz], yside).start()
        core_s(y, zz)

    def core_a(q):
        def send(zz):
            copy(ga.at[c, q, zz], ga.at[c, q, zz], ca_s, ca_r, core).start()

        return send

    def core_b(yy, zz):
        copy(gb.at[c, yy, zz], gb.at[c, yy, zz], cb_s, cb_r, core).start()

    def core_s(yy, zz):
        copy(sb.at[yy, zz, c], sb.at[yy, zz, c], cs_s, cs_r.at[yy], core).start()

    def got_a(q):
        def wait(zz):
            copy(ga.at[c, q, zz], ga.at[c, q, zz], ra_s, ra_r.at[q, zz], here).wait_recv()

        return wait

    def got_b(zz):
        copy(gb.at[c, y, zz], gb.at[c, y, zz], rb_s, rb_r.at[zz], here).wait_recv()

    def got_s(zz):
        copy(sb.at[y, zz, c], sb.at[y, zz, c], rs_s, rs_r.at[zz], here).wait_recv()

    def got_yb(zz):
        copy(gb.at[c, oy, zz], gb.at[c, oy, zz], yb_s, yb_r.at[zz], here).wait_recv()
        core_b(oy, zz)

    def got_ys(zz):
        copy(sb.at[oy, zz, c], sb.at[oy, zz, c], ys_s, ys_r.at[zz], here).wait_recv()
        core_s(oy, zz)

    copy(qa.at[:3], qa.at[:3], q_s.at[0], q_r.at[0], here).wait_recv()
    copy(qb.at[:3], qb.at[:3], q_s.at[1], q_r.at[1], here).wait_recv()
    for s in range(NQ):
        mix[KD * s:KD * (s + 1), :NA] = qa[s].astype(F32)
        mix[KD * s:KD * (s + 1), NA:] = qb[s].astype(F32)
    for q in range(NC):
        ga[c, q, z] = mix[:40, 256 * q:256 * (q + 1)].astype(BF16)
    gb[c, y, z] = mix[:40, NA:].astype(BF16)

    for q in range(NC):
        ring_a(q)(z, right)
        ring_a(q)(z, left)
        core_a(q)(z)
    ring_b(z, right)
    ring_b(z, left)
    side_b(z)

    @pl.when(far)
    def _():
        copy(sb.at[y, z, c], sb.at[y, z, c], sw_s, sw_r, here).wait_recv()

    ring_s(z, right)
    ring_s(z, left)
    side_s(z)

    def hop(t, got, ring, side, last):
        zr = (z - t + NZ) % NZ
        zl = (z + t) % NZ
        for zz, device, reach in ((zr, right, 8 if last == 0 else 7), (zl, left, 8 if last == 1 else 7)):
            @pl.when(t <= reach)
            def _():
                got(zz)

                @pl.when(t < reach)
                def _():
                    ring(zz, device)

                side(zz)

    def side_hop(t, got):
        got((z - t + NZ) % NZ)

        @pl.when((t > 0) & (t < 8))
        def _():
            got((z + t) % NZ)

    def step(s, _):
        @pl.when(s <= 8)
        def _():
            for q in range(NC):
                hop(s, got_a(q), ring_a(q), core_a(q), q % 2)
            hop(s, got_b, ring_b, side_b, 0)
            hop(s, got_s, ring_s, side_s, 1)

        @pl.when(s >= YLAG)
        def _():
            side_hop(s - YLAG, got_yb)
            side_hop(s - YLAG, got_ys)

        return 0

    def grad_part(col):
        copy(sb.at[col, :, oc], sb.at[col, :, oc], cs_s, cs_r.at[col], here).wait_recv()
        prod = None
        for zz in range(4):
            lhs = jnp.concatenate(
                [jnp.concatenate([sb[col, 4 * b + zz, cc] for b in range(4)], axis=0) for cc in range(2)], axis=1
            )
            term = lax.dot_general(
                lhs, grads[:, 256 * zz:256 * (zz + 1)], (((1,), (1,)), ((), ())), preferred_element_type=F32
            )
            prod = term if prod is None else prod + term
        for b in range(4):
            snd_g[4 * col + b] = prod[128 * b:128 * (b + 1), :].astype(BF16)
        for k in (2, 1, 3, 0):
            to = 4 * col + (m % 4 + k) % 4

            @pl.when(to != m)
            def _():
                copy(snd_g.at[to], rcv_g.at[m], xg_s, xg_r, {"dp": d, "mp": to}).start()

            @pl.when(to == m)
            def _():
                rcv_g[m] = snd_g[to]

    def act_part(off, piece, width):
        lhs = piece[...].reshape(NZ * 40, width)
        return lax.dot_general(
            lhs, acts[:, off:off + width], (((1,), (1,)), ((), ())), preferred_element_type=F32
        )

    def act_first():
        get_a.wait()
        copy(ga.at[oc], ga.at[oc], ca_s, ca_r, here).wait_recv()
        acc[...] = act_part(0, ga.at[0, 0], 256)
        for cc in range(2):
            for q in range(NC):
                if cc or q:
                    acc[...] += act_part(cc * HALF + 256 * q, ga.at[cc, q], 256)

    def act_rest():
        copy(gb.at[oc], gb.at[oc], cb_s, cb_r, here).wait_recv()
        for cc in range(2):
            for yy in range(2):
                acc[...] += act_part(cc * HALF + NA + yy * NB, gb.at[cc, yy], NB)
        for mm in range(NM):
            yy, z0 = mm // 4, 4 * (mm % 4)
            for i in range(4):
                src = 40 * (z0 + i) + 20 * yy
                mix[20 * i:20 * (i + 1), :256] = acc[src:src + 20, :]
            snd_a[mm] = mix[:KM, :256].astype(BF16)
        for t in range(1, NM):
            to = (m + t) % NM
            copy(snd_a.at[to], rcv_a.at[m], xa_s, xa_r, {"dp": d, "mp": to}).start()
        rcv_a[m] = snd_a[m]


    lax.fori_loop(1, 9, step, 0)
    act_first()
    lax.fori_loop(9, 9 + YLAG, step, 0)
    get_g.wait()
    grad_part(1 - m // 4)
    grad_part(m // 4)
    act_rest()

    copy(rcv_g.at[:7], rcv_g.at[:7], xg_s, xg_r, here).wait_recv()
    total = rcv_g[0].astype(F32)
    for s in range(1, NM):
        total += rcv_g[s].astype(F32)
    g_t = total.astype(BF16)
    for i in range(8):
        own_g[i % 2, 16 * (i // 2):16 * (i // 2 + 1), :] = g_t[16 * i:16 * (i + 1), :]
    mine_g = c * NM + m
    for t in range(1, NM):
        to = (m + t) % NM
        copy(own_g.at[c], gt.at[mine_g], gt_s, gt_r, {"dp": d, "mp": to}).start()
        copy(own_g.at[oc], gt.at[mine_g], gt_s, gt_r, {"dp": d_other, "mp": to}).start()
    copy(own_g.at[oc], gt.at[mine_g], gt_s, gt_r, core).start()
    gt[mine_g] = own_g[c]
    copy(rcv_a.at[:7], rcv_a.at[:7], xa_s, xa_r, here).wait_recv()
    total = rcv_a[0].astype(F32)
    for s in range(1, NM):
        total += rcv_a[s].astype(F32)
    act[c, :KM, :] = total.astype(BF16)
    copy(act.at[c, :KM], act.at[c, :KM], ac_s, ac_r, core).start()
    copy(act.at[oc, :KM], act.at[oc, :KM], ac_s, ac_r, here).wait_recv()

    copy(gt.at[:15], gt.at[:15], gt_s, gt_r, here).wait_recv()

    nt = (((1,), (1,)), ((), ()))
    groups = [(z // 4 + q) % 4 for q in (2, 1, 3, 0)]
    squares = [(act[cc].astype(F32) ** 2).astype(BF16) for cc in range(2)]

    def rows(*pieces):
        return jnp.concatenate(
            [jnp.zeros((q, 256), BF16) if isinstance(q, int) else q for q in pieces], axis=0
        )

    for half in (oy, y):
        full = jnp.zeros((256, 128), F32)
        rest = jnp.zeros((128, 128), F32)
        for cc in range(2):
            a_sq = squares[cc]
            g_val = gt[pl.ds(cc * NM + 4 * half, 4)].reshape(256, 256)
            g_sq = (g_val.astype(F32) ** 2).astype(BF16)
            parts = g_sq.reshape(NZ, 2, 8, 256)
            full += lax.dot_general(g_val, act[cc], nt, preferred_element_type=F32)
            full += lax.dot_general(g_sq, rows(KM, a_sq[:48]), nt, preferred_element_type=F32)
            rest += lax.dot_general(
                parts[:, 0].reshape(128, 256), rows(a_sq[48:KM], 96), nt, preferred_element_type=F32
            )
            rest += lax.dot_general(
                parts[:, 1].reshape(128, 256), rows(32, a_sq[48:KM], 64), nt, preferred_element_type=F32
            )
        part[half, :, :16] = full.astype(BF16).reshape(NZ, 16, 128)
        part[half, :, 16:] = rest.astype(BF16).reshape(NZ, 8, 128)
        if half is oy:
            for q, g in enumerate(groups):
                mine = pl.ds(4 * g, 4)
                copy(part.at[oy, mine], r1.at[mine], p1_s, p1_r.at[q], yside).start()
    for q, g in enumerate(groups):
        mine = pl.ds(4 * g, 4)
        copy(r1.at[:4], r1.at[:4], p1_s, p1_r.at[q], here).wait_recv()
        p2[mine] = (part[y, mine].astype(F32) + r1[mine].astype(F32)).astype(BF16)
        for i in range(4):
            to = 4 * g + i

            @pl.when(to != z)
            def _():
                copy(p2.at[to], r2.at[z], p2_s, p2_r, dev(y, to, c)).start()
    r2[z] = p2[z]
    copy(r2.at[:15], r2.at[:15], p2_s, p2_r, here).wait_recv()
    total = r2[0].astype(F32)
    for s in range(1, NZ):
        total += r2[s].astype(F32)
    last = jnp.concatenate([total[16:, :32], total[16:, 32:64]], axis=0)
    diag = jnp.concatenate([total[:16, KM:], last], axis=1) / tokens_all
    diag_t[...] = diag
    scaled = total[:16, :KM] / (diag + damping[0])
    sc[y, z, c] = jnp.concatenate([scaled, jnp.zeros((16, 128 - KM), F32)], axis=1).astype(BF16)

    for t in range(1, NZ):
        copy(sc.at[y, z, c], sc.at[y, z, c], sz_s, sz_r.at[z // 4], dev(y, (z + t) % NZ, c)).start()
    groups = [(z // 4 + q) % 4 for q in (0, 1, 3, 2)]
    for q, g in enumerate(groups):
        mine = pl.ds(4 * g, 4)
        width = 4 if q else 3
        copy(sc.at[0, :width, 0], sc.at[0, :width, 0], sz_s, sz_r.at[g], here).wait_recv()
        for yy, cc in quad:
            copy(sc.at[y, mine, c], sc.at[y, mine, c], sq_s, sq_r, dev(yy, z, cc)).start()
    copy(bo.at[:7], bo.at[:7], bo_s, bo_r, here).wait_recv()
    copy(sc.at[:, :12], sc.at[:, :12], sq_s, sq_r, here).wait_recv()

    total = jnp.zeros((128, 128), F32)
    for mm in range(NM):
        yy, z0 = mm // 4, 4 * (mm % 4)
        total += jnp.dot(bo[mm], sc[yy, z0:z0 + 4].reshape(128, 128), preferred_element_type=F32)
    bk[m] = total.T[:KM, :].astype(BF16)
    for t in range(1, NM):
        copy(bk.at[m], bk.at[m], bk_s, bk_r, {"dp": d, "mp": (m + t) % NM}).start()
    copy(bk.at[:7], bk.at[:7], bk_s, bk_r, here).wait_recv()
    for mm in range(NM):
        yy, z0 = mm // 4, 4 * (mm % 4)
        b_val = bk[mm].astype(F32)
        for i in range(4):
            dst = 40 * (z0 + i) + 20 * yy
            bf[dst:dst + 20, :] = b_val[20 * i:20 * (i + 1), :]
    back_t = bf[...].T.astype(BF16)
    for cc in range(2):
        for off, piece, width in (
            *((cc * HALF + 256 * q, ga.at[cc, q], 256) for q in range(NC)),
            (cc * HALF + NA, gb.at[cc, 0], NB),
            (cc * HALF + NA + NB, gb.at[cc, 1], NB),
        ):
            rhs = piece[...].reshape(NZ * 40, width)
            up = jnp.dot(back_t, rhs, preferred_element_type=F32)
            update[off:off + width, :] = up.T.astype(BF16)

    @pl.when(far)
    def _():
        copy(bt, bt, sw_s, sw_r, here).wait_send()

    def sent(ref, ssem):
        copy(ref, ref, ssem, sw_r, here).wait_send()

    sent(qa.at[:3], q_s.at[0])
    sent(qb.at[:3], q_s.at[1])
    sent(bo.at[:7], bo_s)
    sent(snd_a.at[:7], xa_s)
    sent(snd_g.at[:7], xg_s)
    sent(gt.at[:15], gt_s)
    sent(act.at[0, :KM], ac_s)
    sent(bk.at[:7], bk_s)
    sent(r1, p1_s)
    sent(p2.at[:15], p2_s)
    sent(sc.at[0, :15, 0], sz_s)
    sent(sc.at[:, :12], sq_s)
    sent(ga.at[0, :, :15], ra_s)
    sent(gb.at[0, 0, :15], rb_s)
    sent(sb.at[0, :15, 0], rs_s)
    sent(gb.at[0, 0], yb_s)
    sent(sb.at[0, :, 0], ys_s)
    sent(ga.at[0], ca_s)
    sent(gb.at[0], cb_s)
    sent(sb.at[:, :, 0], cs_s)


def solution(mesh):
    def on_device(acts, grads, basis_in, basis_out, damping):
        tokens_all = acts.shape[0] * mesh.shape["dp"]
        vmem = pl.BlockSpec(memory_space=pltpu.VMEM)
        dma = pltpu.SemaphoreType.DMA
        v = pltpu.VMEM

        def hbm(array):
            return pltpu.with_memory_space_constraint(array, pltpu.MemorySpace.HBM)

        def body(*refs):
            kernel(tokens_all, *refs)

        update, diag_t = pl.pallas_call(
            body,
            out_shape=(
                jax.ShapeDtypeStruct((3584, 128), BF16),
                jax.ShapeDtypeStruct((16, KM), F32),
            ),
            in_specs=[pl.BlockSpec(memory_space=pltpu.MemorySpace.HBM)] * 4 + [pl.BlockSpec(memory_space=pltpu.SMEM)],
            out_specs=(vmem, vmem),
            scratch_shapes=[
                v(acts.shape, BF16), v(grads.shape, BF16), v((KD, acts.shape[1]), BF16),
                v((NQ, KD, NA), BF16), v((NQ, KD, NB), BF16), v((KM, NA + NB), F32),
                v((2, NC, NZ, 40, 256), BF16), v((2, 2, NZ, 40, NB), BF16),
                v((2, NZ, 2, 128, 128), BF16), v((NM, 128, 128), BF16), v((128, 128), BF16), v((640, 256), F32),
                v((NM, KM, 256), BF16), v((NM, 128, 256), BF16),
                v((NM, KM, 256), BF16), v((NM, 128, 256), BF16),
                v((2, 128, 256), BF16), v((2, 64, 256), BF16), v((2 * NM, 64, 256), BF16),
                v((2, NZ, 24, 128), BF16), v((NZ, 24, 128), BF16),
                v((NZ, 24, 128), BF16), v((NZ, 24, 128), BF16),
                v((2, NZ, 2, 16, 128), BF16), v((NM, KM, 128), BF16), v((640, 128), F32),
                dma((2,)), dma((2,)), dma, dma((NC, NZ)), dma, dma((NZ,)), dma, dma((NZ,)),
                dma, dma((NZ,)), dma, dma((NZ,)),
                dma, dma, dma, dma, dma, dma((2,)), dma, dma, dma, dma,
                dma, dma, dma, dma, dma, dma,
                dma, dma((4,)), dma, dma,
                dma, dma((4,)), dma, dma, dma, dma, dma((6,)), dma, dma,
            ],
            compiler_params=pltpu.CompilerParams(
                collective_id=0, has_side_effects=True, vmem_limit_bytes=40 * 2**20
            ),
        )(hbm(acts), hbm(grads), hbm(basis_in.T), hbm(basis_out), damping)
        return update, diag_t.T

    placed = (P("dp", "mp"), P("dp", "mp"), P("mp", "dp"), P("dp", "mp"), P())
    return jax.shard_map(
        on_device,
        mesh=mesh,
        in_specs=placed,
        out_specs=(P("mp", "dp"), P("mp", "dp")),
        check_vma=False,
    )
```

```python
import jax
import jax.numpy as jnp
from jax import lax
from jax.experimental import pallas as pl
from jax.experimental.pallas import tpu as pltpu
from jax.sharding import PartitionSpec as P

F32 = jnp.float32
BF16 = jnp.bfloat16
MESH = pl.DeviceIdType.MESH

NZ = 16
NQ = 4
NM = 8
KD = 10
KM = 80
NA = 1024
NB = 384
HALF = NA + 2 * NB
NC = 4
YLAG = 2


def kernel(
    tokens_all,
    acts_h, grads_h, bin_t, bout, damping,
    update, diag_t,
    acts, grads, bin_v,
    qa, qb, mix, ga, gb, sb, bo, bt, acc,
    snd_a, snd_g, rcv_a, rcv_g, act, own_g, gt, part, r1, p2, r2, sc, bk, bf,
    q_s, q_r, ra_s, ra_r, rb_s, rb_r, yb_s, yb_r, rs_s, rs_r, ys_s, ys_r,
    ca_s, ca_r, cb_s, cb_r, cs_s, cs_r, sw_s, sw_r, bo_s, bo_r,
    xa_s, xa_r, xg_s, xg_r, gt_s, gt_r, p1_s, p1_r, p2_s, p2_r,
    sz_s, sz_r, sq_s, sq_r, bk_s, bk_r, in_s, ac_s, ac_r,
):
    d = lax.axis_index("dp")
    m = lax.axis_index("mp")
    y = d // 32
    z = (d // 2) % 16
    c = d % 2
    oy = 1 - y
    oc = 1 - c
    me_q = 2 * y + c
    d_other = d + 1 - 2 * c

    def dev(yy, zz, cc):
        return {"dp": yy * 32 + zz * 2 + cc, "mp": m}

    def copy(src, dst, ssem, rsem, device):
        return pltpu.make_async_remote_copy(
            src_ref=src, dst_ref=dst, send_sem=ssem, recv_sem=rsem,
            device_id=device, device_id_type=MESH,
        )

    here = {"dp": d, "mp": m}
    right = dev(y, (z + 1) % NZ, c)
    left = dev(y, (z + NZ - 1) % NZ, c)
    core = dev(y, z, oc)
    yside = dev(oy, z, c)
    quad = [(y, oc), (oy, c), (oy, oc)]
    peers = [
        4 * ((m // 4 + a) % 2) + (m % 4 + b) % 4
        for a, b in ((1, 2), (1, 1), (1, 3), (1, 0), (0, 2), (0, 1), (0, 3))
    ]
    swap_a = d // 8
    swap_d = 8 * m + d % 8
    far = swap_a != m

    act[:, KM:, :] = jnp.zeros((2, 128 - KM, 256), BF16)
    barrier = pltpu.get_barrier_semaphore()

    def greet(device):
        pl.semaphore_signal(barrier, inc=1, device_id=device, device_id_type=MESH)

    for t in range(1, NZ):
        greet(dev(y, (z + t) % NZ, c))
    for yy, cc in quad:
        greet(dev(yy, z, cc))
    for t in range(1, NM):
        greet({"dp": d, "mp": (m + t) % NM})
        greet({"dp": d_other, "mp": (m + t) % NM})

    @pl.when(far)
    def _():
        greet({"dp": swap_d, "mp": swap_a})

    a_off = pl.multiple_of(c * HALF, 128)
    b_off = pl.multiple_of(c * HALF + NA + y * NB, 128)
    get_b = pltpu.make_async_copy(bin_t, bin_v, in_s.at[0])
    own_o = pltpu.make_async_copy(bout, bo.at[m], in_s.at[2])
    get_g = pltpu.make_async_copy(grads_h, grads, in_s.at[4])
    get_a = pltpu.make_async_copy(acts_h, acts, in_s.at[5])
    own_o.start()
    get_b.start()

    get_g.start()
    get_a.start()
    own_o.wait()
    bt[...] = bo[m].astype(F32).T.astype(BF16)
    get_b.wait()
    qa[me_q] = bin_v[:, pl.ds(a_off, NA)]
    qb[me_q] = bin_v[:, pl.ds(b_off, NB)]

    @pl.when(jnp.logical_not(far))
    def _():
        sb[y, z, c] = bt[...]

    pl.semaphore_wait(barrier, NZ - 1 + 3 + 2 * (NM - 1) + far.astype(jnp.int32))

    @pl.when(far)
    def _():
        copy(bt, sb.at[swap_d // 32, (swap_d // 2) % 16, swap_d % 2], sw_s, sw_r,
             {"dp": swap_d, "mp": swap_a}).start()

    for yy, cc in quad:
        a_to = pl.multiple_of(cc * HALF, 128)
        b_to = pl.multiple_of(cc * HALF + NA + yy * NB, 128)
        copy(bin_v.at[:, pl.ds(a_to, NA)], qa.at[me_q], q_s.at[0], q_r.at[0], dev(yy, z, cc)).start()
        copy(bin_v.at[:, pl.ds(b_to, NB)], qb.at[me_q], q_s.at[1], q_r.at[1], dev(yy, z, cc)).start()
    for to in peers:
        copy(bout, bo.at[m], bo_s, bo_r, {"dp": d, "mp": to}).start()

    def ring_a(q):
        def send(zz, device):
            copy(ga.at[c, q, zz], ga.at[c, q, zz], ra_s, ra_r.at[q, zz], device).start()

        return send

    def ring_b(zz, device):
        copy(gb.at[c, y, zz], gb.at[c, y, zz], rb_s, rb_r.at[zz], device).start()

    def ring_s(zz, device):
        copy(sb.at[y, zz, c], sb.at[y, zz, c], rs_s, rs_r.at[zz], device).start()

    def side_b(zz):
        copy(gb.at[c, y, zz], gb.at[c, y, zz], yb_s, yb_r.at[zz], yside).start()
        core_b(y, zz)

    def side_s(zz):
        copy(sb.at[y, zz, c], sb.at[y, zz, c], ys_s, ys_r.at[zz], yside).start()
        core_s(y, zz)

    def core_a(q):
        def send(zz):
            copy(ga.at[c, q, zz], ga.at[c, q, zz], ca_s, ca_r, core).start()

        return send

    def core_b(yy, zz):
        copy(gb.at[c, yy, zz], gb.at[c, yy, zz], cb_s, cb_r, core).start()

    def core_s(yy, zz):
        copy(sb.at[yy, zz, c], sb.at[yy, zz, c], cs_s, cs_r.at[yy], core).start()

    def got_a(q):
        def wait(zz):
            copy(ga.at[c, q, zz], ga.at[c, q, zz], ra_s, ra_r.at[q, zz], here).wait_recv()

        return wait

    def got_b(zz):
        copy(gb.at[c, y, zz], gb.at[c, y, zz], rb_s, rb_r.at[zz], here).wait_recv()

    def got_s(zz):
        copy(sb.at[y, zz, c], sb.at[y, zz, c], rs_s, rs_r.at[zz], here).wait_recv()

    def got_yb(zz):
        copy(gb.at[c, oy, zz], gb.at[c, oy, zz], yb_s, yb_r.at[zz], here).wait_recv()
        core_b(oy, zz)

    def got_ys(zz):
        copy(sb.at[oy, zz, c], sb.at[oy, zz, c], ys_s, ys_r.at[zz], here).wait_recv()
        core_s(oy, zz)

    copy(qa.at[:3], qa.at[:3], q_s.at[0], q_r.at[0], here).wait_recv()
    copy(qb.at[:3], qb.at[:3], q_s.at[1], q_r.at[1], here).wait_recv()
    for s in range(NQ):
        mix[KD * s:KD * (s + 1), :NA] = qa[s].astype(F32)
        mix[KD * s:KD * (s + 1), NA:] = qb[s].astype(F32)
    for q in range(NC):
        ga[c, q, z] = mix[:40, 256 * q:256 * (q + 1)].astype(BF16)
    gb[c, y, z] = mix[:40, NA:].astype(BF16)

    for q in range(NC):
        ring_a(q)(z, right)
        ring_a(q)(z, left)
        core_a(q)(z)
    ring_b(z, right)
    ring_b(z, left)
    side_b(z)

    @pl.when(far)
    def _():
        copy(sb.at[y, z, c], sb.at[y, z, c], sw_s, sw_r, here).wait_recv()

    ring_s(z, right)
    ring_s(z, left)
    side_s(z)

    def hop(t, got, ring, side, last):
        zr = (z - t + NZ) % NZ
        zl = (z + t) % NZ
        for zz, device, reach in ((zr, right, 8 if last == 0 else 7), (zl, left, 8 if last == 1 else 7)):
            @pl.when(t <= reach)
            def _():
                got(zz)

                @pl.when(t < reach)
                def _():
                    ring(zz, device)

                side(zz)

    def side_hop(t, got):
        got((z - t + NZ) % NZ)

        @pl.when((t > 0) & (t < 8))
        def _():
            got((z + t) % NZ)

    def step(s, _):
        @pl.when(s <= 8)
        def _():
            for q in range(NC):
                hop(s, got_a(q), ring_a(q), core_a(q), q % 2)
            hop(s, got_b, ring_b, side_b, 0)
            hop(s, got_s, ring_s, side_s, 1)

        @pl.when(s >= YLAG)
        def _():
            side_hop(s - YLAG, got_yb)
            side_hop(s - YLAG, got_ys)

        return 0

    def grad_part(col):
        copy(sb.at[col, :, oc], sb.at[col, :, oc], cs_s, cs_r.at[col], here).wait_recv()
        prod = None
        for zz in range(4):
            lhs = jnp.concatenate(
                [jnp.concatenate([sb[col, 4 * b + zz, cc] for b in range(4)], axis=0) for cc in range(2)], axis=1
            )
            term = lax.dot_general(
                lhs, grads[:, 256 * zz:256 * (zz + 1)], (((1,), (1,)), ((), ())), preferred_element_type=F32
            )
            prod = term if prod is None else prod + term
        for b in range(4):
            snd_g[4 * col + b] = prod[128 * b:128 * (b + 1), :].astype(BF16)
        for k in (2, 1, 3, 0):
            to = 4 * col + (m % 4 + k) % 4

            @pl.when(to != m)
            def _():
                copy(snd_g.at[to], rcv_g.at[m], xg_s, xg_r, {"dp": d, "mp": to}).start()

            @pl.when(to == m)
            def _():
                rcv_g[m] = snd_g[to]

    def act_part(off, piece, width):
        lhs = piece[...].reshape(NZ * 40, width)
        return lax.dot_general(
            lhs, acts[:, off:off + width], (((1,), (1,)), ((), ())), preferred_element_type=F32
        )

    def act_first():
        get_a.wait()
        copy(ga.at[oc], ga.at[oc], ca_s, ca_r, here).wait_recv()
        acc[...] = act_part(0, ga.at[0, 0], 256)
        for cc in range(2):
            for q in range(NC):
                if cc or q:
                    acc[...] += act_part(cc * HALF + 256 * q, ga.at[cc, q], 256)

    def act_rest():
        copy(gb.at[oc], gb.at[oc], cb_s, cb_r, here).wait_recv()
        for cc in range(2):
            for yy in range(2):
                acc[...] += act_part(cc * HALF + NA + yy * NB, gb.at[cc, yy], NB)
        for mm in range(NM):
            yy, z0 = mm // 4, 4 * (mm % 4)
            for i in range(4):
                src = 40 * (z0 + i) + 20 * yy
                mix[20 * i:20 * (i + 1), :256] = acc[src:src + 20, :]
            snd_a[mm] = mix[:KM, :256].astype(BF16)
        for to in peers:
            copy(snd_a.at[to], rcv_a.at[m], xa_s, xa_r, {"dp": d, "mp": to}).start()
        rcv_a[m] = snd_a[m]


    lax.fori_loop(1, 9, step, 0)
    act_first()
    lax.fori_loop(9, 9 + YLAG, step, 0)
    get_g.wait()
    grad_part(1 - m // 4)
    grad_part(m // 4)
    act_rest()

    copy(rcv_g.at[:7], rcv_g.at[:7], xg_s, xg_r, here).wait_recv()
    total = rcv_g[0].astype(F32)
    for s in range(1, NM):
        total += rcv_g[s].astype(F32)
    g_t = total.astype(BF16)
    for i in range(8):
        own_g[i % 2, 16 * (i // 2):16 * (i // 2 + 1), :] = g_t[16 * i:16 * (i + 1), :]
    mine_g = c * NM + m
    for to in peers:
        copy(own_g.at[c], gt.at[mine_g], gt_s, gt_r, {"dp": d, "mp": to}).start()
        copy(own_g.at[oc], gt.at[mine_g], gt_s, gt_r, {"dp": d_other, "mp": to}).start()
    copy(own_g.at[oc], gt.at[mine_g], gt_s, gt_r, core).start()
    gt[mine_g] = own_g[c]
    copy(rcv_a.at[:7], rcv_a.at[:7], xa_s, xa_r, here).wait_recv()
    total = rcv_a[0].astype(F32)
    for s in range(1, NM):
        total += rcv_a[s].astype(F32)
    act[c, :KM, :] = total.astype(BF16)
    copy(act.at[c, :KM], act.at[c, :KM], ac_s, ac_r, core).start()
    copy(act.at[oc, :KM], act.at[oc, :KM], ac_s, ac_r, here).wait_recv()

    copy(gt.at[:15], gt.at[:15], gt_s, gt_r, here).wait_recv()

    nt = (((1,), (1,)), ((), ()))
    groups = [(z // 4 + q) % 4 for q in (2, 1, 3, 0)]
    squares = [(act[cc].astype(F32) ** 2).astype(BF16) for cc in range(2)]

    def rows(*pieces):
        return jnp.concatenate(
            [jnp.zeros((q, 256), BF16) if isinstance(q, int) else q for q in pieces], axis=0
        )

    for half in (oy, y):
        full = jnp.zeros((256, 128), F32)
        rest = jnp.zeros((128, 128), F32)
        for cc in range(2):
            a_sq = squares[cc]
            g_val = gt[pl.ds(cc * NM + 4 * half, 4)].reshape(256, 256)
            g_sq = (g_val.astype(F32) ** 2).astype(BF16)
            parts = g_sq.reshape(NZ, 2, 8, 256)
            full += lax.dot_general(g_val, act[cc], nt, preferred_element_type=F32)
            full += lax.dot_general(g_sq, rows(KM, a_sq[:48]), nt, preferred_element_type=F32)
            rest += lax.dot_general(
                parts[:, 0].reshape(128, 256), rows(a_sq[48:KM], 96), nt, preferred_element_type=F32
            )
            rest += lax.dot_general(
                parts[:, 1].reshape(128, 256), rows(32, a_sq[48:KM], 64), nt, preferred_element_type=F32
            )
        part[half, :, :16] = full.astype(BF16).reshape(NZ, 16, 128)
        part[half, :, 16:] = rest.astype(BF16).reshape(NZ, 8, 128)
        if half is oy:
            for q, g in enumerate(groups):
                mine = pl.ds(4 * g, 4)
                copy(part.at[oy, mine], r1.at[mine], p1_s, p1_r.at[q], yside).start()
    for q, g in enumerate(groups):
        mine = pl.ds(4 * g, 4)
        copy(r1.at[:4], r1.at[:4], p1_s, p1_r.at[q], here).wait_recv()
        p2[mine] = (part[y, mine].astype(F32) + r1[mine].astype(F32)).astype(BF16)
        for i in range(4):
            to = 4 * g + i

            @pl.when(to != z)
            def _():
                copy(p2.at[to], r2.at[z], p2_s, p2_r, dev(y, to, c)).start()
    r2[z] = p2[z]
    copy(r2.at[:15], r2.at[:15], p2_s, p2_r, here).wait_recv()
    total = r2[0].astype(F32)
    for s in range(1, NZ):
        total += r2[s].astype(F32)
    last = jnp.concatenate([total[16:, :32], total[16:, 32:64]], axis=0)
    diag = jnp.concatenate([total[:16, KM:], last], axis=1) / tokens_all
    diag_t[...] = diag
    scaled = total[:16, :KM] / (diag + damping[0])
    sc[y, z, c] = jnp.concatenate([scaled, jnp.zeros((16, 128 - KM), F32)], axis=1).astype(BF16)

    for t in (8, 7, 9, 6, 10, 5, 11, 4, 12, 3, 13, 2, 14, 1, 15):
        copy(sc.at[y, z, c], sc.at[y, z, c], sz_s, sz_r.at[z // 4], dev(y, (z + t) % NZ, c)).start()
    groups = [(z // 4 + q) % 4 for q in (2, 1, 3, 0)]
    for q, g in enumerate(groups):
        mine = pl.ds(4 * g, 4)
        width = 4 if q < 3 else 3
        copy(sc.at[0, :width, 0], sc.at[0, :width, 0], sz_s, sz_r.at[g], here).wait_recv()
        for yy, cc in quad:
            copy(sc.at[y, mine, c], sc.at[y, mine, c], sq_s, sq_r, dev(yy, z, cc)).start()
    copy(bo.at[:7], bo.at[:7], bo_s, bo_r, here).wait_recv()
    copy(sc.at[:, :12], sc.at[:, :12], sq_s, sq_r, here).wait_recv()

    total = jnp.zeros((128, 128), F32)
    for mm in range(NM):
        yy, z0 = mm // 4, 4 * (mm % 4)
        total += jnp.dot(bo[mm], sc[yy, z0:z0 + 4].reshape(128, 128), preferred_element_type=F32)
    bk[m] = total.T[:KM, :].astype(BF16)
    for to in peers:
        copy(bk.at[m], bk.at[m], bk_s, bk_r, {"dp": d, "mp": to}).start()
    copy(bk.at[:7], bk.at[:7], bk_s, bk_r, here).wait_recv()
    for mm in range(NM):
        yy, z0 = mm // 4, 4 * (mm % 4)
        b_val = bk[mm].astype(F32)
        for i in range(4):
            dst = 40 * (z0 + i) + 20 * yy
            bf[dst:dst + 20, :] = b_val[20 * i:20 * (i + 1), :]
    back_t = bf[...].T.astype(BF16)
    for cc in range(2):
        for off, piece, width in (
            *((cc * HALF + 256 * q, ga.at[cc, q], 256) for q in range(NC)),
            (cc * HALF + NA, gb.at[cc, 0], NB),
            (cc * HALF + NA + NB, gb.at[cc, 1], NB),
        ):
            rhs = piece[...].reshape(NZ * 40, width)
            up = jnp.dot(back_t, rhs, preferred_element_type=F32)
            update[off:off + width, :] = up.T.astype(BF16)

    @pl.when(far)
    def _():
        copy(bt, bt, sw_s, sw_r, here).wait_send()

    def sent(ref, ssem):
        copy(ref, ref, ssem, sw_r, here).wait_send()

    sent(qa.at[:3], q_s.at[0])
    sent(qb.at[:3], q_s.at[1])
    sent(bo.at[:7], bo_s)
    sent(snd_a.at[:7], xa_s)
    sent(snd_g.at[:7], xg_s)
    sent(gt.at[:15], gt_s)
    sent(act.at[0, :KM], ac_s)
    sent(bk.at[:7], bk_s)
    sent(r1, p1_s)
    sent(p2.at[:15], p2_s)
    sent(sc.at[0, :15, 0], sz_s)
    sent(sc.at[:, :12], sq_s)
    sent(ga.at[0, :, :15], ra_s)
    sent(gb.at[0, 0, :15], rb_s)
    sent(sb.at[0, :15, 0], rs_s)
    sent(gb.at[0, 0], yb_s)
    sent(sb.at[0, :, 0], ys_s)
    sent(ga.at[0], ca_s)
    sent(gb.at[0], cb_s)
    sent(sb.at[:, :, 0], cs_s)


def solution(mesh):
    def on_device(acts, grads, basis_in, basis_out, damping):
        tokens_all = acts.shape[0] * mesh.shape["dp"]
        vmem = pl.BlockSpec(memory_space=pltpu.VMEM)
        dma = pltpu.SemaphoreType.DMA
        v = pltpu.VMEM

        def hbm(array):
            return pltpu.with_memory_space_constraint(array, pltpu.MemorySpace.HBM)

        def body(*refs):
            kernel(tokens_all, *refs)

        update, diag_t = pl.pallas_call(
            body,
            out_shape=(
                jax.ShapeDtypeStruct((3584, 128), BF16),
                jax.ShapeDtypeStruct((16, KM), F32),
            ),
            in_specs=[pl.BlockSpec(memory_space=pltpu.MemorySpace.HBM)] * 4 + [pl.BlockSpec(memory_space=pltpu.SMEM)],
            out_specs=(vmem, vmem),
            scratch_shapes=[
                v(acts.shape, BF16), v(grads.shape, BF16), v((KD, acts.shape[1]), BF16),
                v((NQ, KD, NA), BF16), v((NQ, KD, NB), BF16), v((KM, NA + NB), F32),
                v((2, NC, NZ, 40, 256), BF16), v((2, 2, NZ, 40, NB), BF16),
                v((2, NZ, 2, 128, 128), BF16), v((NM, 128, 128), BF16), v((128, 128), BF16), v((640, 256), F32),
                v((NM, KM, 256), BF16), v((NM, 128, 256), BF16),
                v((NM, KM, 256), BF16), v((NM, 128, 256), BF16),
                v((2, 128, 256), BF16), v((2, 64, 256), BF16), v((2 * NM, 64, 256), BF16),
                v((2, NZ, 24, 128), BF16), v((NZ, 24, 128), BF16),
                v((NZ, 24, 128), BF16), v((NZ, 24, 128), BF16),
                v((2, NZ, 2, 16, 128), BF16), v((NM, KM, 128), BF16), v((640, 128), F32),
                dma((2,)), dma((2,)), dma, dma((NC, NZ)), dma, dma((NZ,)), dma, dma((NZ,)),
                dma, dma((NZ,)), dma, dma((NZ,)),
                dma, dma, dma, dma, dma, dma((2,)), dma, dma, dma, dma,
                dma, dma, dma, dma, dma, dma,
                dma, dma((4,)), dma, dma,
                dma, dma((4,)), dma, dma, dma, dma, dma((6,)), dma, dma,
            ],
            compiler_params=pltpu.CompilerParams(
                collective_id=0, has_side_effects=True, vmem_limit_bytes=40 * 2**20
            ),
        )(hbm(acts), hbm(grads), hbm(basis_in.T), hbm(basis_out), damping)
        return update, diag_t.T

    placed = (P("dp", "mp"), P("dp", "mp"), P("mp", "dp"), P("dp", "mp"), P())
    return jax.shard_map(
        on_device,
        mesh=mesh,
        in_specs=placed,
        out_specs=(P("mp", "dp"), P("mp", "dp")),
        check_vma=False,
    )
```
